32 devices in a mesh: dp: 4 (over z), shard: 8 (over y, x, core).
Axes of the slice: x: 2, y: 2, z: 4, core: 2. Of those that a mesh axis runs over, the one named last changes fastest.
Arguments:
- tokens: bfloat16 [16384, 1024], P(('dp', 'shard')), may hold values from -6 to 6
- targets: bfloat16 [16384, 1024], P(('dp', 'shard')), may hold values from -6 to 6
- segments: int32 [16384], P('dp'), may hold values from 0 to 511, as said below
- valid: int32 [16384], P(('dp', 'shard')), may hold values from 0 to 1, as said below
- master: float32 [1024, 12288], P('shard')
- vectors: float32 [13312], P('shard')
- left_stat: float32 [8, 96, 128, 128], P('shard'), as said below
- right_stat: float32 [8, 96, 128, 128], P('shard'), as said below
- left_root: bfloat16 [8, 96, 128, 128], P('shard'), as said below
- right_root: bfloat16 [8, 96, 128, 128], P('shard'), as said below
- vector_stat: float32 [13312], P('shard'), may hold values from 0.01 to 1
Outputs:
- input_grad: float32 [16384, 1024], P(('dp', 'shard'))
- grad_norm: float32 [], replicated
- new_left: float32 [8, 96, 128, 128], P('shard')
- new_right: float32 [8, 96, 128, 128], P('shard')
- new_master: float32 [1024, 12288], P('shard')
- master_copy: bfloat16 [1024, 12288], P('shard')
- new_vectors: float32 [13312], P('shard')
- new_vector_stat: float32 [13312], P('shard')
The draws below stay inside these ranges and needn't reach their ends.
Inputs may be any that keep to these rules, and one draw needn't show every extreme that they name: `segments`: taken in order of positions, within each sequence the numbers start at 0 and never fall, rising by at most one from a position to the next; positions 128 to 384 lie in one document, and so do positions 640 to 896. The row of position 0 of every sequence is valid. `left_stat`: every block is symmetric. `right_stat`: every block is symmetric. `left_root`: every block is symmetric. `right_root`: every block is symmetric.
All inputs are finite; a program needn't handle non-finite values.
Results may differ from the reference program's by a relative error of at most 0.012.
Values may be sent and summed in bfloat16 or wider, within the bound.
A program may use at most 320 MiB of HBM per device.

```python
import math
from functools import partial
import jax
import jax.numpy as jnp
from jax import lax

D = 1024
HD = 64
ROT = 16
FF = 4096
BS = 128
SEQ_LEN = 1024
TOKENS = 16384
SEQS = 16
W = 12288
VLEN = 13312


def draw_segments(key, part):
    key = jax.random.fold_in(key, 101)
    rate_key, flag_key = jax.random.split(key)
    rate_level = jax.random.randint(rate_key, (SEQS, 1), 2, 9)
    rate_level = jnp.where(jnp.arange(SEQS)[:, None] == 0, 0, rate_level)
    bit_draws = jax.random.randint(flag_key, (SEQS, SEQ_LEN), 0, 256)
    doc_starts = bit_draws % jnp.left_shift(1, rate_level) == 0
    position_row = jnp.arange(SEQ_LEN)[None, :]
    quarter = SEQ_LEN // 4
    eighth = SEQ_LEN // 8
    zone_one = (position_row > quarter - eighth) & (position_row <= quarter + eighth)
    zone_two = (position_row > 3 * quarter - eighth) & (position_row <= 3 * quarter + eighth)
    quiet_zone = (position_row == 0) | zone_one | zone_two
    start_flags = jnp.where(quiet_zone, 0, doc_starts.astype(jnp.int32))
    by_position = jnp.cumsum(start_flags, axis=1).astype(jnp.int32)
    by_rows = by_position.reshape(SEQS, 4, quarter)[:, jnp.array([0, 3, 1, 2])]
    return by_rows.reshape(TOKENS)


def draw_valid(key, part):
    key = jax.random.fold_in(key, 202)
    row_index = jnp.arange(TOKENS)
    sequence = row_index // SEQ_LEN
    threshold = 250 + 500 * sequence // max(SEQS - 1, 1)
    picks = jax.random.randint(key, (TOKENS,), 0, 1000)
    return jnp.where((picks < threshold) | (row_index % SEQ_LEN == 0), 1, 0).astype(jnp.int32)


def draw_master(key, part):
    key = jax.random.fold_in(key, 303)
    column = jnp.arange(W)
    scale = jnp.where(column < 3 * D, D ** (-0.5), jnp.where(column < 4 * D, 4.0 * D ** (-0.5), jnp.where(column < 4 * D + FF, D ** (-0.5), FF ** (-0.5))))
    return jax.random.normal(key, (D, W), jnp.float32) * scale[None, :]


def draw_vectors(key, part):
    key = jax.random.fold_in(key, 404)
    entry = jnp.arange(VLEN)
    is_gain = (entry < D) | (entry >= 2 * D) & (entry < 3 * D)
    noise = jax.random.normal(key, (VLEN,), jnp.float32)
    return jnp.where(is_gain, 1.0 + 0.1 * noise, 0.2 * noise)


def symmetric_blocks(key, diag_low, diag_high, off_scale):
    first_key, second_key = jax.random.split(key)
    block_shape = (D // BS, W // BS, BS, BS)
    raw_draw = jax.random.normal(first_key, block_shape, jnp.float32)
    symmetric = (raw_draw + jnp.swapaxes(raw_draw, -1, -2)) * (off_scale / math.sqrt(2.0))
    diagonal = jax.random.uniform(second_key, block_shape[:-1], jnp.float32, diag_low, diag_high)
    identity = jnp.eye(BS, dtype=bool)
    return jnp.where(identity, diagonal[..., None], symmetric)


def draw_left_stat(key, part):
    return symmetric_blocks(jax.random.fold_in(key, 505), 0.6, 2.0, 0.025)


def draw_right_stat(key, part):
    return symmetric_blocks(jax.random.fold_in(key, 606), 0.6, 2.0, 0.025)


def draw_left_root(key, part):
    return symmetric_blocks(jax.random.fold_in(key, 707), 0.6, 1.6, 0.025).astype(jnp.bfloat16)


def draw_right_root(key, part):
    return symmetric_blocks(jax.random.fold_in(key, 808), 0.6, 1.6, 0.025).astype(jnp.bfloat16)


def block_levels(rng, dims, shards, smallest, largest):
    level = 1.0
    for dim, parts in shards:
        steps = jax.random.uniform(jax.random.fold_in(jax.random.fold_in(rng, 6), dim), (parts,), jnp.float32, smallest / len(shards), largest / len(shards))
        level = level * jnp.repeat(jnp.exp(steps), dims[dim] // parts).reshape((-1,) + (1,) * (len(dims) - 1 - dim))
    return level


def gaussian(stream_key, dims, width, reach, shards=(), held_as=jnp.bfloat16):
    factor_of = block_levels(stream_key, dims, shards, -0.22, 0.18) if shards else 1.0
    values = jax.random.normal(stream_key, dims, jnp.float32) * width * factor_of
    return jnp.minimum(jnp.maximum(values, -reach), reach).astype(held_as)


def setup_inputs(seed: int = 0) -> dict:
    key_of = jax.random.split(jax.random.key(seed), 12)
    return {
        "tokens": gaussian(key_of[0], (TOKENS, D), 1.0, 6.0, ((0, 32),)),
        "targets": gaussian(key_of[1], (TOKENS, D), 1.0, 6.0, ((0, 32),)),
        "segments": draw_segments(jax.random.fold_in(key_of[11], 71), 0),
        "valid": draw_valid(jax.random.fold_in(key_of[11], 71), 0),
        "master": draw_master(jax.random.fold_in(key_of[11], 71), 0),
        "vectors": draw_vectors(jax.random.fold_in(key_of[11], 71), 0),
        "left_stat": draw_left_stat(jax.random.fold_in(key_of[11], 71), 0),
        "right_stat": draw_right_stat(jax.random.fold_in(key_of[11], 71), 0),
        "left_root": draw_left_root(jax.random.fold_in(key_of[11], 71), 0),
        "right_root": draw_right_root(jax.random.fold_in(key_of[11], 71), 0),
        "vector_stat": jnp.clip(jnp.exp(math.log(1.0) - 4.6051702 * jax.random.uniform(key_of[10], (VLEN,), jnp.float32) ** block_levels(key_of[10], (VLEN,), ((0, 8),), -0.2, 0.2)), 0.01, 1.0),
    }


@jax.custom_vjp
def low(v):
    return lax.optimization_barrier(v.astype(jnp.bfloat16)).astype(jnp.float32)

@jax.custom_vjp
def low_back(v):
    return v

def low_keep(v):
    return (low(v), None)

def low_pass(kept, grad):
    return (grad,)

def back_keep(v):
    return (v, None)

def back_low(kept, grad):
    return (low(grad),)
low.defvjp(low_keep, low_pass)
low_back.defvjp(back_keep, back_low)
EPS = 1e-05
NEG = -1e+30
LEARN = 0.5
LEARN_VEC = 0.15
HIGHEST = lax.Precision.HIGHEST

def layer_norm(values, gain, shift):
    row_mean = lax.optimization_barrier(jnp.mean(values, axis=-1, keepdims=True))
    centred = values - row_mean
    spread = lax.optimization_barrier(jnp.mean(centred * centred, axis=-1, keepdims=True))
    return centred * lax.rsqrt(spread + EPS) * gain + shift

def rotate(values, cosine_grid, sine_grid):
    half_rot = ROT // 2
    first = values[..., :half_rot]
    second = values[..., half_rot:ROT]
    return jnp.concatenate([first * cosine_grid - second * sine_grid, second * cosine_grid + first * sine_grid, values[..., ROT:]], axis=-1)

def reorder(values, order):
    shape = values.shape
    quarters = values.reshape(shape[0], 4, SEQ_LEN // 4, *shape[2:])
    return quarters[:, order].reshape(shape)

def run_block(inputs, doc_rows, weights, params):
    group_count = inputs.shape[0]
    row_total = group_count * SEQ_LEN
    in_order = reorder(inputs, [0, 2, 3, 1])
    doc_ids = reorder(doc_rows, [0, 2, 3, 1])
    flat_rows = in_order.reshape(row_total, D)
    norm_one = layer_norm(flat_rows, params[0:D], params[D:2 * D])
    norm_two = layer_norm(flat_rows, params[2 * D:3 * D], params[3 * D:4 * D])
    projected = low_back(jnp.dot(low(norm_one), weights[:, :3 * D], precision=HIGHEST) + params[4 * D:7 * D])
    head_shape = (group_count, SEQ_LEN, D // HD, HD)
    half_rot = ROT // 2
    frequency = jnp.power(10000.0, -2.0 * jnp.arange(half_rot, dtype=jnp.float32) / ROT)
    angle_grid = jnp.arange(SEQ_LEN, dtype=jnp.int32).astype(jnp.float32)[:, None] * frequency[None, :]
    cosine_grid = jnp.cos(angle_grid)[None, :, None, :]
    sine_grid = jnp.sin(angle_grid)[None, :, None, :]
    query_rows = low(rotate(projected[:, :D].reshape(head_shape), cosine_grid, sine_grid))
    key_rows = low(rotate(projected[:, D:2 * D].reshape(head_shape), cosine_grid, sine_grid))
    value_rows = low(projected[:, 2 * D:].reshape(head_shape))
    raw_scores = jnp.einsum('bqhe,bkhe->bhqk', query_rows, key_rows, precision=HIGHEST) * HD ** (-0.5)
    scores = low_back(raw_scores)
    position = jnp.arange(SEQ_LEN, dtype=jnp.int32)
    allowed = (position[None, :] <= position[:, None])[None] & (doc_ids[:, :, None] == doc_ids[:, None, :])
    scores = jnp.where(allowed[:, None], scores, NEG)
    row_max = lax.optimization_barrier(jnp.max(scores, axis=-1, keepdims=True))
    exponent = jnp.exp(scores - row_max)
    soft_weights = exponent / lax.optimization_barrier(jnp.sum(exponent, axis=-1, keepdims=True))
    attention = jnp.einsum('bhqk,bkhe->bqhe', low(soft_weights), value_rows, precision=HIGHEST).reshape(row_total, D)
    attention = low(low_back(attention))
    branch = jnp.dot(attention, weights[:, 3 * D:4 * D], precision=HIGHEST) + params[7 * D:8 * D]
    up_value = low_back(jnp.dot(low(norm_two), weights[:, 4 * D:4 * D + FF], precision=HIGHEST) + params[8 * D:8 * D + FF])
    active = jax.nn.gelu(up_value, approximate=False)
    feed_out = jnp.dot(low(active), weights[:, 4 * D + FF:].T, precision=HIGHEST) + params[8 * D + FF:]
    result = (flat_rows + low_back(branch + feed_out)).reshape(inputs.shape)
    return reorder(result, [0, 3, 1, 2])

def run_layer(inputs, weights, params, segments):
    group_size = math.gcd(SEQS, max(1, 4096 // SEQ_LEN))
    stacked = inputs.reshape(SEQS // group_size, group_size, SEQ_LEN, D)
    doc_stack = segments.reshape(SEQS // group_size, group_size, SEQ_LEN)
    block_step = jax.checkpoint(run_block)
    outputs = lax.map(lambda block_pair: block_step(block_pair[0], block_pair[1], weights, params), (stacked, doc_stack))
    return outputs.reshape(TOKENS, D)

def round_keep(values):
    return lax.optimization_barrier(values.astype(jnp.bfloat16)).astype(jnp.float32)

def reference(tokens, targets, segments, valid, master, vectors, left_stat, right_stat, left_root, right_root, vector_stat):
    weights = lax.optimization_barrier(master.astype(jnp.bfloat16)).astype(jnp.float32)
    params = lax.optimization_barrier(vectors.astype(jnp.bfloat16)).astype(jnp.float32)
    inputs = tokens.astype(jnp.float32)
    outputs, pullback = jax.vjp(partial(run_layer, segments=segments), inputs, weights, params)
    valid_float = valid.astype(jnp.float32)
    valid_total = jnp.sum(valid_float)
    grad_out = TOKENS / valid_total * valid_float[:, None] * (outputs - targets.astype(jnp.float32))
    grad_in, grad_w, grad_v = pullback(grad_out)
    grad_norm = jnp.sqrt(jnp.sum(grad_w * grad_w) + jnp.sum(grad_v * grad_v))
    factor = jnp.minimum(1.0, math.sqrt(D * W / BS) / grad_norm)
    tiles = (grad_w * factor).reshape(D // BS, BS, W // BS, BS)
    new_left = 0.5 * left_stat + 0.5 * jnp.einsum('iajb,icjb->ijac', tiles, tiles, precision=HIGHEST)
    new_right = 0.5 * right_stat + 0.5 * jnp.einsum('iajb,iajd->ijbd', tiles, tiles, precision=HIGHEST)
    tiles_low = round_keep(tiles)
    left_mixed = round_keep(jnp.einsum('ijac,icjd->iajd', left_root.astype(jnp.float32), tiles_low, precision=HIGHEST))
    update = jnp.einsum('iajd,ijdb->iajb', left_mixed, right_root.astype(jnp.float32), precision=HIGHEST).reshape(D, W)
    new_master = master - LEARN * update
    scaled_vec = grad_v * factor
    new_vstat = 0.5 * vector_stat + 0.5 * scaled_vec * scaled_vec
    new_vectors = vectors - LEARN_VEC * scaled_vec / jnp.sqrt(new_vstat)
    return (grad_in, grad_norm, new_left, new_right, new_master, new_master.astype(jnp.bfloat16), new_vectors, new_vstat)
```

```python
from functools import partial
import math

import jax
import jax.numpy as jnp
from jax import lax
from jax.experimental import pallas as pl
from jax.experimental.pallas import tpu as pltpu
from jax.sharding import PartitionSpec as P

HD = 64
ROT = 16
BS = 128
LANES = 128
EPS = 1e-05
NEG = -1e30
BIG = 3e38
LEARN = 0.5
LEARN_VEC = 0.15
F32 = jnp.float32
BF16 = jnp.bfloat16
MIB = 1 << 20


def dot(a, b, dims=((1,), (0,))):
    return lax.dot_general(a, b, (dims, ((), ())), preferred_element_type=F32)


def dot_nt(a, b):
    return dot(a, b, ((1,), (1,)))


def call(kernel, grid, in_specs, out_specs, out_shape, scratch=(), vmem=48, prefetch=0, cost=None):
    return pl.pallas_call(
        kernel,
        out_shape=out_shape,
        grid_spec=pltpu.PrefetchScalarGridSpec(
            num_scalar_prefetch=prefetch,
            grid=grid,
            in_specs=in_specs,
            out_specs=out_specs,
            scratch_shapes=list(scratch),
        ),
        compiler_params=pltpu.CompilerParams(
            vmem_limit_bytes=vmem * MIB, dimension_semantics=("arbitrary",) * len(grid)
        ),
        cost_estimate=cost,
    )


def cost(flops, nbytes, trans=0):
    return pl.CostEstimate(flops=int(flops), bytes_accessed=int(nbytes), transcendentals=int(trans))


def whole(shape):
    rank = len(shape)
    return pl.BlockSpec(shape, lambda *g: (0,) * rank)


def sds(shape, dtype):
    return jax.ShapeDtypeStruct(shape, dtype)


def normed(x):
    mean = jnp.mean(x, axis=-1, keepdims=True)
    centred = x - mean
    rstd = lax.rsqrt(jnp.mean(centred * centred, axis=-1, keepdims=True) + EPS)
    return centred * rstd, rstd


def turn(values, c, lo, hi):
    return values * c + pltpu.roll(values, LANES - ROT // 2, 1) * lo + pltpu.roll(values, ROT // 2, 1) * hi


def pre_kernel(x_ref, vec_ref, w_ref, b_ref, c_ref, lo_ref, hi_ref, n1t_ref, n2_ref, n2t_ref, q_ref, kv_ref, n1_ref):
    j = pl.program_id(0)
    rows, width = x_ref.shape
    step = 128

    @pl.when(j == 0)
    def _():
        def chunk(i, carry):
            at = pl.ds(pl.multiple_of(i * step, step), step)
            xh, _ = normed(x_ref[at, :].astype(F32))
            one = (xh * vec_ref[0:1, :] + vec_ref[1:2, :]).astype(BF16)
            two = (xh * vec_ref[2:3, :] + vec_ref[3:4, :]).astype(BF16)
            n1_ref[at, :] = one
            n2_ref[at, :] = two
            n1t_ref[:, at] = one.T
            n2t_ref[:, at] = two.T
            return carry

        lax.fori_loop(0, rows // step, chunk, 0)

    cols = w_ref.shape[1]
    proj = dot(n1_ref[...], w_ref[...]) + b_ref[...]

    def emit(out, turned):
        for g in range(cols // LANES):
            part = proj[:, g * LANES : (g + 1) * LANES]
            if turned:
                part = turn(part, c_ref[...], lo_ref[...], hi_ref[...])
            out[:, g * LANES : (g + 1) * LANES] = part.astype(BF16)

    nq = width // cols

    @pl.when(j < nq)
    def _():
        emit(q_ref, True)

    @pl.when((j >= nq) & (j < 2 * nq))
    def _():
        emit(kv_ref, True)

    @pl.when(j >= 2 * nq)
    def _():
        emit(kv_ref, False)


def pre(x, vec4, w, b, tables):
    rows, width = x.shape
    cols = 512
    steps = 3 * width // cols
    nq = width // cols
    return call(
        pre_kernel,
        (steps,),
        [
            whole((rows, width)),
            whole(vec4.shape),
            pl.BlockSpec((width, cols), lambda j: (0, j)),
            pl.BlockSpec((1, cols), lambda j: (0, j)),
            whole((rows, LANES)),
            whole((rows, LANES)),
            whole((rows, LANES)),
        ],
        [
            whole((width, rows)),
            whole((rows, width)),
            whole((width, rows)),
            pl.BlockSpec((rows, cols), lambda j: (0, jnp.minimum(j, nq - 1))),
            pl.BlockSpec((rows, cols), lambda j: (0, jnp.maximum(j - nq, 0))),
        ],
        [
            sds((width, rows), BF16),
            sds((rows, width), BF16),
            sds((width, rows), BF16),
            sds((rows, width), BF16),
            sds((rows, 2 * width), BF16),
        ],
        [pltpu.VMEM((rows, width), BF16)],
        cost=cost(6 * rows * width * width, 2 * (3 * width * width + 7 * rows * width)),
    )(x, vec4, w, b, *tables)


def place_keys(own_ref, other_ref, out_ref, parity):
    half = own_ref.shape[0] // 2
    for ref, who in ((own_ref, parity), (other_ref, 1 - parity)):
        for b in range(2):
            quarter = who if b == 0 else 3 - who
            out_ref[pl.ds(pl.multiple_of(quarter * half, half), half), :] = ref[b * half : (b + 1) * half, :]


def att_fwd_kernel(par_ref, q_ref, k_ref, v_ref, ko_ref, vo_ref, qseg_ref, kseg_ref, o_ref, ot_ref, lse_ref, mask, kpos, vpos, sc):
    rows = q_ref.shape[0]
    half = rows // 2
    parity = par_ref[0]
    lane = lax.broadcasted_iota(jnp.int32, (half, LANES), 1)

    @pl.when(pl.program_id(0) == 0)
    def _():
        for b in range(2):
            quarter = parity if b == 0 else 3 - parity

            def one(j, carry):
                qpos = quarter * half + lax.broadcasted_iota(jnp.int32, (half, half), 0)
                kpos_ = j * half + lax.broadcasted_iota(jnp.int32, (half, half), 1)
                same = qseg_ref[b * half : (b + 1) * half, :] == kseg_ref[pl.ds(j, 1), :]
                mask[b, j] = jnp.where((kpos_ <= qpos) & same, BIG, NEG)
                return carry

            lax.fori_loop(0, 4, one, 0)
        for j in range(4):
            vpos[j * half : (j + 1) * half, LANES:] = jnp.ones((half, LANES), BF16)

    place_keys(k_ref, ko_ref, kpos, parity)
    place_keys(v_ref, vo_ref, vpos.at[:, 0:LANES], parity)
    for b in range(2):
        quarter = parity if b == 0 else 3 - parity
        at = slice(b * half, (b + 1) * half)
        both = q_ref[at, :] * jnp.asarray(HD**-0.5, BF16)
        outs = []
        for h in range(2):
            mine = (lane < HD) if h == 0 else (lane >= HD)
            qh = jnp.where(mine, both, jnp.zeros_like(both))

            def score(j, top):
                keys = kpos[pl.ds(pl.multiple_of(j * half, half), half), :]
                s = jnp.minimum(dot_nt(qh, keys), mask[b, j])
                sc[j] = s
                for g in range(half // LANES):
                    top = jnp.maximum(top, s[:, g * LANES : (g + 1) * LANES])
                return top

            top = lax.fori_loop(0, quarter + 1, score, jnp.full((half, LANES), NEG, F32))
            top = jnp.broadcast_to(jnp.max(top, axis=1, keepdims=True), (half, LANES))
            top_wide = jnp.concatenate([top] * (half // LANES), axis=1)

            def weigh(j, acc):
                p = jnp.exp(sc[j] - top_wide).astype(BF16)
                return acc + dot(p, vpos[pl.ds(pl.multiple_of(j * half, half), half), :])

            acc = lax.fori_loop(0, quarter + 1, weigh, jnp.zeros((half, 2 * LANES), F32))
            den = acc[:, LANES:]
            outs.append(acc[:, :LANES] / den)
            lse = top + jnp.log(den)
            lse_ref[0, h : h + 1, at] = lse.T[0:1, :]
        out = jnp.where(lane < HD, outs[0], outs[1]).astype(BF16)
        o_ref[at, :] = out
        ot_ref[0, :, at] = out.T


def att_fwd(parity, q, kv, kvo, qseg, kseg):
    rows, width = q.shape
    pairs = width // LANES
    half = rows // 2
    col = lambda off: pl.BlockSpec((rows, LANES), lambda p, r: (0, p + off))
    return call(
        att_fwd_kernel,
        (pairs,),
        [col(0), col(0), col(pairs), col(0), col(pairs), whole((rows, 1)), whole((4, half))],
        [
            col(0),
            pl.BlockSpec((1, LANES, rows), lambda p, r: (p, 0, 0)),
            pl.BlockSpec((1, 2, rows), lambda p, r: (p, 0, 0)),
        ],
        [sds((rows, width), BF16), sds((pairs, LANES, rows), BF16), sds((pairs, 2, rows), F32)],
        [
            pltpu.VMEM((2, 4, half, half), F32),
            pltpu.VMEM((2 * rows, LANES), BF16),
            pltpu.VMEM((2 * rows, 2 * LANES), BF16),
            pltpu.VMEM((4, half, half), F32),
        ],
        prefetch=1,
        cost=cost(4 * rows * 2 * rows * width, 2 * 8 * rows * width, 2 * rows * rows * width // HD),
    )(parity, q, kv, kv, kvo, kvo, qseg, kseg)


def att_bwd_kernel(
    par_ref, q_ref, k_ref, v_ref, ko_ref, vo_ref, g_ref, o_ref, lse_ref, qseg_ref, kseg_ref, c_ref, lo_ref, hi_ref,
    dq_ref, dk_ref, dv_ref, dko_ref, dvo_ref, mask, kpos, vpos, dkpos, dvpos,
):
    rows = q_ref.shape[0]
    half = rows // 2
    parity = par_ref[0]
    lane = lax.broadcasted_iota(jnp.int32, (half, LANES), 1)
    lane_k = lane

    @pl.when(pl.program_id(0) == 0)
    def _():
        for b in range(2):
            quarter = parity if b == 0 else 3 - parity

            def one(j, carry):
                kp = j * half + lax.broadcasted_iota(jnp.int32, (half, half), 0)
                qp = quarter * half + lax.broadcasted_iota(jnp.int32, (half, half), 1)
                same = kseg_ref[pl.ds(pl.multiple_of(j * half, half), half), :] == qseg_ref[b : b + 1, :]
                mask[b, j] = jnp.where((kp <= qp) & same, BIG, NEG)
                return carry

            lax.fori_loop(0, 4, one, 0)

    place_keys(k_ref, ko_ref, kpos, parity)
    place_keys(v_ref, vo_ref, vpos, parity)
    dkpos[...] = jnp.zeros_like(dkpos)
    dvpos[...] = jnp.zeros_like(dvpos)
    scale = HD**-0.5
    for b in range(2):
        quarter = parity if b == 0 else 3 - parity
        at = slice(b * half, (b + 1) * half)
        qs = q_ref[at, :] * jnp.asarray(scale, BF16)
        gs = g_ref[at, :]
        prod = (gs.astype(F32) * o_ref[at, :].astype(F32)).T
        zero = jnp.zeros_like(qs)
        parts = []
        for h in range(2):
            mine = (lane < HD) if h == 0 else (lane >= HD)
            qh = jnp.where(mine, qs, zero)
            gh = jnp.where(mine, gs, zero)
            lse = lse_ref[0, h : h + 1, at]
            delta = jnp.sum(prod[h * HD : (h + 1) * HD, :], axis=0, keepdims=True)

            def tile(j, acc):
                ks = pl.ds(pl.multiple_of(j * half, half), half)
                keys = kpos[ks, :]
                s = jnp.minimum(dot_nt(keys, qh), mask[b, j])
                p = jnp.exp(s - lse)
                dp = dot_nt(vpos[ks, :], gh)
                ds = (p * (dp - delta)).astype(BF16)
                dvpos[ks, :] += dot(p.astype(BF16), gh)
                dkpos[ks, :] += dot(ds, qh)
                return acc + dot(ds, keys, ((0,), (0,)))

            parts.append(lax.fori_loop(0, quarter + 1, tile, jnp.zeros((half, LANES), F32)))
        dq = jnp.where(lane < HD, parts[0], parts[1]) * scale
        dq_ref[at, :] = turn(dq, c_ref[at, :], -lo_ref[at, :], -hi_ref[at, :]).astype(BF16)
    for src, mine, theirs in ((dkpos, dk_ref, dko_ref), (dvpos, dv_ref, dvo_ref)):
        for b in range(2):
            at = slice(b * half, (b + 1) * half)
            own = parity if b == 0 else 3 - parity
            other = 1 - parity if b == 0 else 2 + parity
            mine[at, :] = src[pl.ds(pl.multiple_of(own * half, half), half), :].astype(mine.dtype)
            theirs[at, :] = src[pl.ds(pl.multiple_of(other * half, half), half), :].astype(BF16)


def att_bwd(parity, q, kv, kvo, gob, ob, lse, qseg, kseg, tables):
    rows, width = q.shape
    pairs = width // LANES
    half = rows // 2
    col = lambda off: pl.BlockSpec((rows, LANES), lambda p, r: (0, p + off))
    out = sds((rows, width), F32)
    low = sds((rows, width), BF16)
    return call(
        att_bwd_kernel,
        (pairs,),
        [
            col(0), col(0), col(pairs), col(0), col(pairs), col(0), col(0),
            pl.BlockSpec((1, 2, rows), lambda p, r: (p, 0, 0)),
            whole((2, half)), whole((2 * rows, 1)),
            whole((rows, LANES)), whole((rows, LANES)), whole((rows, LANES)),
        ],
        [col(0)] * 5,
        [low, out, out, low, low],
        [
            pltpu.VMEM((2, 4, half, half), F32),
            pltpu.VMEM((2 * rows, LANES), BF16),
            pltpu.VMEM((2 * rows, LANES), BF16),
            pltpu.VMEM((2 * rows, LANES), F32),
            pltpu.VMEM((2 * rows, LANES), F32),
        ],
        prefetch=1,
        cost=cost(10 * rows * 2 * rows * width, 2 * 16 * rows * width, 2 * rows * rows * width // HD),
    )(parity, q, kv, kv, kvo, kvo, gob, ob, lse, qseg, kseg, *tables)


def up_kernel(n2_ref, w_ref, b_ref, h_ref, dg_ref):
    u_all = dot(n2_ref[...], w_ref[...]) + b_ref[...]
    for g in range(u_all.shape[1] // LANES):
        at = slice(g * LANES, (g + 1) * LANES)
        u = u_all[:, at]
        cdf = 0.5 * (1.0 + lax.erf(u * (1.0 / math.sqrt(2.0))))
        h_ref[:, at] = (u * cdf).astype(BF16)
        pdf = jnp.exp(-0.5 * u * u) * (1.0 / math.sqrt(2.0 * math.pi))
        dg_ref[:, at] = (cdf + u * pdf).astype(BF16)


def up(n2, w, b):
    rows, width = n2.shape
    hidden = w.shape[1]
    cols = 512
    blk = pl.BlockSpec((rows, cols), lambda j: (0, j))
    return call(
        up_kernel,
        (hidden // cols,),
        [whole((rows, width)), pl.BlockSpec((width, cols), lambda j: (0, j)), pl.BlockSpec((1, cols), lambda j: (0, j))],
        [blk, blk],
        [sds((rows, hidden), BF16), sds((rows, hidden), BF16)],
        cost=cost(2 * rows * width * hidden, 2 * (width * hidden + 2 * rows * hidden), 2 * rows * hidden),
    )(n2, w, b)


def out_kernel(ob_ref, hb_ref, wo_ref, wd_ref, bo_ref, bd_ref, x_ref, t_ref, valid_ref, gy_ref, gb_ref, gbt_ref, sum_ref):
    branch = dot(ob_ref[...], wo_ref[...]) + bo_ref[...]
    feed = dot_nt(hb_ref[...], wd_ref[...]) + bd_ref[...]
    y = x_ref[...].astype(F32) + (branch + feed)
    g = valid_ref[...] * (y - t_ref[...].astype(F32))
    low = g.astype(BF16)
    gy_ref[...] = g
    gb_ref[...] = low
    gbt_ref[...] = low.T
    sum_ref[...] = jnp.sum(low.astype(F32), axis=0, keepdims=True)


def out_grad(ob, hb, wo, wd, bo, bd, x, t, valid):
    rows, width = ob.shape
    hidden = hb.shape[1]
    cols = 256
    col = pl.BlockSpec((rows, cols), lambda j: (0, j))
    vec = pl.BlockSpec((1, cols), lambda j: (0, j))
    return call(
        out_kernel,
        (width // cols,),
        [
            whole((rows, width)), whole((rows, hidden)),
            pl.BlockSpec((width, cols), lambda j: (0, j)), pl.BlockSpec((cols, hidden), lambda j: (j, 0)),
            vec, vec, col, col, whole((rows, 1)),
        ],
        [col, col, pl.BlockSpec((cols, rows), lambda j: (j, 0)), vec],
        [sds((rows, width), F32), sds((rows, width), BF16), sds((width, rows), BF16), sds((1, width), F32)],
        cost=cost(2 * rows * width * (width + hidden), 2 * (width * (width + hidden) + 6 * rows * width)),
    )(ob, hb, wo, wd, bo, bd, x, t, valid)


def dgrad_kernel(gb_ref, wo_ref, wd_ref, wu_ref, dg_ref, gob_ref, gub_ref, sum_ref, gn2_ref):
    @pl.when(pl.program_id(0) == 0)
    def _():
        gob_ref[...] = dot_nt(gb_ref[...], wo_ref[...]).astype(BF16)
        gn2_ref[...] = jnp.zeros_like(gn2_ref)

    act = dot(gb_ref[...], wd_ref[...])
    gub = (act * dg_ref[...].astype(F32)).astype(BF16)
    gub_ref[...] = gub
    sum_ref[...] = jnp.sum(gub.astype(F32), axis=0, keepdims=True)
    gn2_ref[...] += dot_nt(gub, wu_ref[...])


def dgrad(gb, wo, wd, wu, dg):
    rows, width = gb.shape
    hidden = dg.shape[1]
    cols = 512
    blk = pl.BlockSpec((rows, cols), lambda j: (0, j))
    wblk = pl.BlockSpec((width, cols), lambda j: (0, j))
    return call(
        dgrad_kernel,
        (hidden // cols,),
        [whole((rows, width)), whole((width, width)), wblk, wblk, blk],
        [whole((rows, width)), blk, pl.BlockSpec((1, cols), lambda j: (0, j)), whole((rows, width))],
        [sds((rows, width), BF16), sds((rows, hidden), BF16), sds((1, hidden), F32), sds((rows, width), F32)],
        cost=cost(2 * rows * width * (width + 2 * hidden), 2 * (width * (width + 2 * hidden) + 6 * rows * width)),
    )(gb, wo, wd, wu, dg)


def last_kernel(
    dq_ref, dk_ref, dv_ref, dko_ref, dvo_ref, c_ref, lo_ref, hi_ref, w_ref, x_ref, vec_ref, gn2_ref, gy_ref, scale_ref,
    gqkv_ref, in_ref, vg_ref, sum_ref, gn1,
):
    j = pl.program_id(0)
    rows, width = x_ref.shape
    cols = w_ref.shape[1]
    nq = width // cols

    @pl.when(j == 0)
    def _():
        gn1[...] = jnp.zeros_like(gn1)

    @pl.when(j < nq)
    def _():
        gqkv_ref[...] = dq_ref[...]

    @pl.when((j >= nq) & (j < 2 * nq))
    def _():
        for g in range(cols // LANES):
            at = slice(g * LANES, (g + 1) * LANES)
            grad = dk_ref[:, at] + dko_ref[:, at].astype(F32)
            gqkv_ref[:, at] = turn(grad, c_ref[...], -lo_ref[...], -hi_ref[...]).astype(BF16)

    @pl.when(j >= 2 * nq)
    def _():
        gqkv_ref[...] = (dv_ref[...] + dvo_ref[...].astype(F32)).astype(BF16)

    low = gqkv_ref[...]
    sum_ref[...] = jnp.sum(low.astype(F32), axis=0, keepdims=True)
    gn1[...] += dot_nt(low, w_ref[...])

    @pl.when(j == 3 * nq - 1)
    def _():
        step = 64
        vg_ref[...] = jnp.zeros_like(vg_ref)
        scale = scale_ref[0, 0]

        def chunk(i, carry):
            at = pl.ds(pl.multiple_of(i * step, step), step)
            xh, rstd = normed(x_ref[at, :].astype(F32))
            total = gy_ref[at, :]
            sums = []
            for g_n, gain in ((gn1[at, :], vec_ref[0:1, :]), (gn2_ref[at, :], vec_ref[2:3, :])):
                sums.append(jnp.sum(g_n * xh, axis=0, keepdims=True))
                sums.append(jnp.sum(g_n, axis=0, keepdims=True))
                e = g_n * gain
                mean = jnp.mean(e, axis=-1, keepdims=True)
                along = jnp.mean(e * xh, axis=-1, keepdims=True)
                total = total + rstd * (e - mean - xh * along)
            in_ref[at, :] = total * scale
            vg_ref[...] += jnp.concatenate(sums, axis=0)
            return carry

        lax.fori_loop(0, rows // step, chunk, 0)


def last(dq, dk, dv, dko, dvo, tables, w, x, vec4, gn2, gy, scale):
    rows, width = x.shape
    cols = 512
    nq = width // cols
    at = lambda lo: pl.BlockSpec((rows, cols), lambda j: (0, jnp.clip(j - lo * nq, 0, nq - 1)))
    return call(
        last_kernel,
        (3 * nq,),
        [
            at(0), at(1), at(2), at(1), at(2),
            whole((rows, LANES)), whole((rows, LANES)), whole((rows, LANES)),
            pl.BlockSpec((width, cols), lambda j: (0, j)),
            whole((rows, width)), whole(vec4.shape), whole((rows, width)), whole((rows, width)),
            pl.BlockSpec(memory_space=pltpu.SMEM),
        ],
        [
            pl.BlockSpec((rows, cols), lambda j: (0, j)), whole((rows, width)), whole((4, width)),
            pl.BlockSpec((1, cols), lambda j: (0, j)),
        ],
        [sds((rows, 3 * width), BF16), sds((rows, width), F32), sds((4, width), F32), sds((1, 3 * width), F32)],
        [pltpu.VMEM((rows, width), F32)],
        cost=cost(6 * rows * width * width, 2 * (3 * width * width + 20 * rows * width)),
    )(dq, dk, dv, dko, dvo, *tables, w, x, vec4, gn2, gy, scale)


def wgrad_kernel(core_ref, a_ref, ao_ref, b_ref, bo_ref, out_ref):
    blocks, size = a_ref.shape[0], a_ref.shape[2]
    tokens = a_ref.shape[3]
    a = a_ref[...].reshape(blocks * size, tokens)
    ao = ao_ref[...].reshape(blocks * size, tokens)
    out_ref[...] = (dot(a, b_ref[...]) + dot(ao, bo_ref[...])).astype(BF16)


def wgrad(core, at_own, at_other, b_own, b_other):
    width, tokens = at_own.shape
    blocks = width // (2 * BS)
    total = b_own.shape[1]
    cols = 512
    return call(
        wgrad_kernel,
        (total // cols,),
        [
            pl.BlockSpec((blocks, 1, BS, tokens), lambda j, c: (0, c[0], 0, 0)),
            whole((blocks, 1, BS, tokens)),
            pl.BlockSpec((tokens, cols), lambda j, c: (0, j)),
            pl.BlockSpec((tokens, cols), lambda j, c: (0, j)),
        ],
        pl.BlockSpec((blocks * BS, cols), lambda j, c: (0, j)),
        sds((blocks * BS, total), BF16),
        prefetch=1,
        cost=cost(2 * tokens * width * total, 2 * total * (2 * tokens + width // 2)),
    )(core, at_own.reshape(blocks, 2, BS, tokens), at_other, b_own, b_other)


def update_kernel(f_ref, g_ref, ls_ref, rs_ref, lr_ref, rr_ref, m_ref, nl_ref, nr_ref, nm_ref, mc_ref):
    factor = f_ref[0, 0]
    half_sq = 0.5 * factor * factor
    for k in range(ls_ref.shape[1]):
        at = slice(k * BS, (k + 1) * BS)
        g = g_ref[:, at]
        gt = g.T
        nl_ref[0, k] = 0.5 * ls_ref[0, k] + half_sq * dot(g, gt)
        nr_ref[0, k] = 0.5 * rs_ref[0, k] + half_sq * dot(gt, g)
        tb = (g.astype(F32) * factor).astype(BF16)
        mb = dot(lr_ref[0, k], tb).astype(BF16)
        new = m_ref[:, at] - LEARN * dot(mb, rr_ref[0, k])
        nm_ref[:, at] = new
        mc_ref[:, at] = new.astype(BF16)


def update(factor, g, ls, rs, lr, rr, m):
    rows, total = g.shape
    count = ls.shape[1]
    per = 8
    blk = pl.BlockSpec((1, per, BS, BS), lambda j: (0, j, 0, 0))
    col = pl.BlockSpec((rows, per * BS), lambda j: (0, j))
    return call(
        update_kernel,
        (count // per,),
        [pl.BlockSpec(memory_space=pltpu.SMEM), col, blk, blk, blk, blk, col],
        [blk, blk, col, col],
        [sds(ls.shape, F32), sds(rs.shape, F32), sds(m.shape, F32), sds(m.shape, BF16)],
        cost=cost(8 * rows * total * BS, rows * total * 32),
    )(factor, g, ls, rs, lr, rr, m)


def angles(positions):
    half_rot = ROT // 2
    frequency = jnp.power(10000.0, -2.0 * jnp.arange(half_rot, dtype=F32) / ROT)
    grid = positions.astype(F32)[:, None] * frequency[None, :]
    cosine, sine = jnp.cos(grid), jnp.sin(grid)
    rows = positions.shape[0]
    ones = jnp.ones((rows, HD - ROT), F32)
    zero = jnp.zeros((rows, HD - ROT), F32)
    blank = jnp.zeros((rows, half_rot), F32)
    c = jnp.concatenate([cosine, cosine, ones] * 2, axis=1)
    lo = jnp.concatenate([-sine, blank, zero] * 2, axis=1)
    hi = jnp.concatenate([blank, sine, zero] * 2, axis=1)
    return c, lo, hi


def body(
    tokens, targets, segments, valid, master, vectors, left_stat, right_stat, left_root, right_root, vector_stat,
):
    rows, width = tokens.shape
    stack = master.shape[1]
    hidden = (stack - 4 * width) // 2
    half = rows // 2
    shards = lax.axis_size("shard")
    replicas = lax.axis_size("dp")
    index = lax.axis_index("shard")
    parity = index % 2
    par = parity.astype(jnp.int32).reshape(1)
    swap = [(i, i ^ 1) for i in range(shards)]
    groups = [[i for i in range(shards) if i % 2 == c] for c in range(2)]

    low = master.astype(BF16)
    w_qkv = lax.all_gather(low[:, : 3 * width], "shard", axis=0, tiled=True)
    w_rest = lax.all_gather(low[:, 3 * width :], "shard", axis=0, tiled=True)
    params = lax.all_gather(vectors.astype(BF16), "shard", axis=0, tiled=True).astype(F32)
    w_out = w_rest[:, :width]
    w_up = w_rest[:, width : width + hidden]
    w_down = w_rest[:, width + hidden :]

    vec4 = params[: 4 * width].reshape(4, width)
    b_qkv = params[4 * width : 7 * width].reshape(1, -1)
    b_out = params[7 * width : 8 * width].reshape(1, -1)
    b_up = params[8 * width : 8 * width + hidden].reshape(1, -1)
    b_down = params[8 * width + hidden :].reshape(1, -1)

    valid_float = valid.astype(F32)
    count = lax.psum(lax.psum(jnp.sum(valid_float), "shard"), "dp")
    scale = rows * shards * replicas / count

    local = jnp.arange(half, dtype=jnp.int32)
    positions = jnp.concatenate([parity * half + local, (3 - parity) * half + local])
    tables = angles(positions)
    start = (index - parity) * rows
    sequence = lax.dynamic_slice_in_dim(segments, start, 2 * rows).reshape(4, half)
    key_seg = jnp.stack([sequence[0], sequence[2], sequence[3], sequence[1]])
    own_seg = lax.dynamic_slice_in_dim(segments, index * rows, rows)

    n1t, n2, n2t, q, kv = pre(tokens, vec4, w_qkv, b_qkv, tables)
    kvo = lax.ppermute(kv, "shard", swap)
    hb, dg = up(n2, w_up, b_up)
    ob, obt, lse = att_fwd(par, q, kv, kvo, own_seg.reshape(rows, 1), key_seg)
    obt = obt.reshape(width, rows)
    gy, gb, gbt, gb_sum = out_grad(
        ob, hb, w_out, w_down, b_out, b_down, tokens, targets, valid_float.reshape(rows, 1)
    )
    gob, gub, gub_sum, gn2 = dgrad(gb, w_out, w_down, w_up, dg)

    other = 1 - parity
    pick = lambda a: lax.dynamic_slice_in_dim(a.reshape(-1, 2, BS, rows), other, 1, axis=1)
    hb_o, gb_o, gub_o, gbt_o, obt_o, n2t_o, n1t_o = (
        lax.ppermute(a, "shard", swap) for a in (hb, gb, gub, pick(gbt), pick(obt), pick(n2t), pick(n1t))
    )
    dw_down = wgrad(par, gbt, gbt_o, hb, hb_o)
    dw_out = wgrad(par, obt, obt_o, gb, gb_o)
    dw_up = wgrad(par, n2t, n2t_o, gub, gub_o)

    def reduce(part):
        part = lax.psum_scatter(part, "shard", scatter_dimension=0, axis_index_groups=groups, tiled=True)
        part = lax.psum_scatter(part, "dp", scatter_dimension=1, tiled=True)
        return lax.all_gather(part, "dp", axis=1, tiled=True)

    g_down, g_out, g_up = reduce(dw_down), reduce(dw_out), reduce(dw_up)

    dq, dk, dv, dk_o, dv_o = att_bwd(
        par, q, kv, kvo, gob, ob, lse, own_seg.reshape(2, half), key_seg.reshape(2 * rows, 1), tables
    )
    dk_r = lax.ppermute(dk_o, "shard", swap)
    dv_r = lax.ppermute(dv_o, "shard", swap)
    gqkv, input_grad, vec_grad, gqkv_sum = last(
        dq, dk, dv, dk_r, dv_r, tables, w_qkv, tokens, vec4, gn2, gy, scale.reshape(1, 1)
    )
    gqkv_o = lax.ppermute(gqkv, "shard", swap)
    g_qkv = reduce(wgrad(par, n1t, n1t_o, gqkv, gqkv_o))

    vector_grad = jnp.concatenate(
        [vec_grad.reshape(-1), gqkv_sum.reshape(-1), gb_sum.reshape(-1), gub_sum.reshape(-1), gb_sum.reshape(-1)]
    )
    vector_grad = lax.psum(lax.psum(vector_grad, "shard"), "dp")
    own_len = vectors.shape[0]
    own_vector = lax.dynamic_slice_in_dim(vector_grad, index * own_len, own_len)

    grads = jnp.concatenate([g_qkv, g_out, g_up, g_down], axis=1)
    square_sum = jnp.sum(jnp.square(grads.astype(F32))) + jnp.sum(own_vector * own_vector)
    grad_norm = scale * jnp.sqrt(lax.psum(square_sum, "shard"))
    factor = scale * jnp.minimum(1.0, math.sqrt(width * stack / BS) / grad_norm)
    new_left, new_right, new_master, master_copy = update(
        factor.reshape(1, 1), grads, left_stat, right_stat, left_root, right_root, master
    )
    scaled_vec = own_vector * factor
    new_vstat = 0.5 * vector_stat + 0.5 * scaled_vec * scaled_vec
    new_vectors = vectors - LEARN_VEC * scaled_vec / jnp.sqrt(new_vstat)
    return (input_grad, grad_norm, new_left, new_right, new_master, master_copy, new_vectors, new_vstat)


def solution(mesh):
    rows = P(("dp", "shard"), None)
    quad = P("shard", None, None, None)
    return jax.shard_map(
        body,
        mesh=mesh,
        in_specs=(
            rows, rows, P("dp"), P(("dp", "shard")), P("shard", None), P("shard"), quad, quad, quad, quad, P("shard"),
        ),
        out_specs=(rows, P(), quad, quad, P("shard", None), P("shard", None), P("shard"), P("shard")),
        check_vma=False,
    )
```

```python
from functools import partial
import math

import jax
import jax.numpy as jnp
from jax import lax
from jax.experimental import pallas as pl
from jax.experimental.pallas import tpu as pltpu
from jax.sharding import PartitionSpec as P

HD = 64
ROT = 16
BS = 128
LANES = 128
EPS = 1e-05
NEG = -1e30
BIG = 3e38
LEARN = 0.5
LEARN_VEC = 0.15
F32 = jnp.float32
BF16 = jnp.bfloat16
MIB = 1 << 20


def dot(a, b, dims=((1,), (0,))):
    return lax.dot_general(a, b, (dims, ((), ())), preferred_element_type=F32)


def dot_nt(a, b):
    return dot(a, b, ((1,), (1,)))


def call(kernel, grid, in_specs, out_specs, out_shape, scratch=(), vmem=48, prefetch=0, cost=None):
    return pl.pallas_call(
        kernel,
        out_shape=out_shape,
        grid_spec=pltpu.PrefetchScalarGridSpec(
            num_scalar_prefetch=prefetch,
            grid=grid,
            in_specs=in_specs,
            out_specs=out_specs,
            scratch_shapes=list(scratch),
        ),
        compiler_params=pltpu.CompilerParams(
            vmem_limit_bytes=vmem * MIB, dimension_semantics=("arbitrary",) * len(grid)
        ),
        cost_estimate=cost,
    )


def cost(flops, nbytes, trans=0):
    return pl.CostEstimate(flops=int(flops), bytes_accessed=int(nbytes), transcendentals=int(trans))


def whole(shape):
    rank = len(shape)
    return pl.BlockSpec(shape, lambda *g: (0,) * rank)


def sds(shape, dtype):
    return jax.ShapeDtypeStruct(shape, dtype)


def normed(x):
    mean = jnp.mean(x, axis=-1, keepdims=True)
    centred = x - mean
    rstd = lax.rsqrt(jnp.mean(centred * centred, axis=-1, keepdims=True) + EPS)
    return centred * rstd, rstd


def turn(values, c, lo, hi):
    return values * c + pltpu.roll(values, LANES - ROT // 2, 1) * lo + pltpu.roll(values, ROT // 2, 1) * hi


def pre_kernel(x_ref, vec_ref, w_ref, b_ref, c_ref, lo_ref, hi_ref, n1t_ref, n2_ref, n2t_ref, q_ref, kv_ref, n1_ref):
    j = pl.program_id(0)
    rows, width = x_ref.shape
    step = 128

    @pl.when(j == 0)
    def _():
        def chunk(i, carry):
            at = pl.ds(pl.multiple_of(i * step, step), step)
            xh, _ = normed(x_ref[at, :].astype(F32))
            one = (xh * vec_ref[0:1, :] + vec_ref[1:2, :]).astype(BF16)
            two = (xh * vec_ref[2:3, :] + vec_ref[3:4, :]).astype(BF16)
            n1_ref[at, :] = one
            n2_ref[at, :] = two
            n1t_ref[:, at] = one.T
            n2t_ref[:, at] = two.T
            return carry

        lax.fori_loop(0, rows // step, chunk, 0)

    cols = w_ref.shape[1]
    proj = dot(n1_ref[...], w_ref[...]) + b_ref[...]

    def emit(out, turned):
        for g in range(cols // LANES):
            part = proj[:, g * LANES : (g + 1) * LANES]
            if turned:
                part = turn(part, c_ref[...], lo_ref[...], hi_ref[...])
            out[:, g * LANES : (g + 1) * LANES] = part.astype(BF16)

    nq = width // cols

    @pl.when(j < nq)
    def _():
        emit(q_ref, True)

    @pl.when((j >= nq) & (j < 2 * nq))
    def _():
        emit(kv_ref, True)

    @pl.when(j >= 2 * nq)
    def _():
        emit(kv_ref, False)


def pre(x, vec4, w, b, tables):
    rows, width = x.shape
    cols = 512
    steps = 3 * width // cols
    nq = width // cols
    return call(
        pre_kernel,
        (steps,),
        [
            whole((rows, width)),
            whole(vec4.shape),
            pl.BlockSpec((width, cols), lambda j: (0, j)),
            pl.BlockSpec((1, cols), lambda j: (0, j)),
            whole((rows, LANES)),
            whole((rows, LANES)),
            whole((rows, LANES)),
        ],
        [
            whole((width, rows)),
            whole((rows, width)),
            whole((width, rows)),
            pl.BlockSpec((rows, cols), lambda j: (0, jnp.minimum(j, nq - 1))),
            pl.BlockSpec((rows, cols), lambda j: (0, jnp.maximum(j - nq, 0))),
        ],
        [
            sds((width, rows), BF16),
            sds((rows, width), BF16),
            sds((width, rows), BF16),
            sds((rows, width), BF16),
            sds((rows, 2 * width), BF16),
        ],
        [pltpu.VMEM((rows, width), BF16)],
        cost=cost(6 * rows * width * width, 2 * (3 * width * width + 7 * rows * width)),
    )(x, vec4, w, b, *tables)


def place_keys(own_ref, other_ref, out_ref, parity):
    half = own_ref.shape[0] // 2
    for ref, who in ((own_ref, parity), (other_ref, 1 - parity)):
        for b in range(2):
            quarter = who if b == 0 else 3 - who
            out_ref[pl.ds(pl.multiple_of(quarter * half, half), half), :] = ref[b * half : (b + 1) * half, :]


def att_fwd_kernel(par_ref, q_ref, k_ref, v_ref, ko_ref, vo_ref, qseg_ref, kseg_ref, o_ref, ot_ref, lse_ref, mask, kpos, vpos, sc):
    rows = q_ref.shape[0]
    half = rows // 2
    parity = par_ref[0]
    lane = lax.broadcasted_iota(jnp.int32, (half, LANES), 1)

    @pl.when(pl.program_id(0) == 0)
    def _():
        for b in range(2):
            quarter = parity if b == 0 else 3 - parity

            def one(j, carry):
                qpos = quarter * half + lax.broadcasted_iota(jnp.int32, (half, half), 0)
                kpos_ = j * half + lax.broadcasted_iota(jnp.int32, (half, half), 1)
                same = qseg_ref[b * half : (b + 1) * half, :] == kseg_ref[pl.ds(j, 1), :]
                mask[b, j] = jnp.where((kpos_ <= qpos) & same, BIG, NEG)
                return carry

            lax.fori_loop(0, 4, one, 0)
        for j in range(4):
            vpos[j * half : (j + 1) * half, LANES:] = jnp.ones((half, LANES), BF16)

    place_keys(k_ref, ko_ref, kpos, parity)
    place_keys(v_ref, vo_ref, vpos.at[:, 0:LANES], parity)
    for b in range(2):
        quarter = parity if b == 0 else 3 - parity
        at = slice(b * half, (b + 1) * half)
        both = q_ref[at, :] * jnp.asarray(HD**-0.5, BF16)
        outs = []
        for h in range(2):
            mine = (lane < HD) if h == 0 else (lane >= HD)
            qh = jnp.where(mine, both, jnp.zeros_like(both))

            def score(j, top):
                keys = kpos[pl.ds(pl.multiple_of(j * half, half), half), :]
                s = jnp.minimum(dot_nt(qh, keys), mask[b, j])
                sc[j] = s
                for g in range(half // LANES):
                    top = jnp.maximum(top, s[:, g * LANES : (g + 1) * LANES])
                return top

            top = lax.fori_loop(0, quarter + 1, score, jnp.full((half, LANES), NEG, F32))
            top = jnp.broadcast_to(jnp.max(top, axis=1, keepdims=True), (half, LANES))
            top_wide = jnp.concatenate([top] * (half // LANES), axis=1)

            def weigh(j, acc):
                p = jnp.exp(sc[j] - top_wide).astype(BF16)
                return acc + dot(p, vpos[pl.ds(pl.multiple_of(j * half, half), half), :])

            acc = lax.fori_loop(0, quarter + 1, weigh, jnp.zeros((half, 2 * LANES), F32))
            den = acc[:, LANES:]
            outs.append(acc[:, :LANES] / den)
            lse = top + jnp.log(den)
            lse_ref[0, h : h + 1, at] = lse.T[0:1, :]
        out = jnp.where(lane < HD, outs[0], outs[1]).astype(BF16)
        o_ref[at, :] = out
        ot_ref[0, :, at] = out.T


def att_fwd(parity, q, kv, kvo, qseg, kseg):
    rows, width = q.shape
    pairs = width // LANES
    half = rows // 2
    col = lambda off: pl.BlockSpec((rows, LANES), lambda p, r: (0, p + off))
    return call(
        att_fwd_kernel,
        (pairs,),
        [col(0), col(0), col(pairs), col(0), col(pairs), whole((rows, 1)), whole((4, half))],
        [
            col(0),
            pl.BlockSpec((1, LANES, rows), lambda p, r: (p, 0, 0)),
            pl.BlockSpec((1, 2, rows), lambda p, r: (p, 0, 0)),
        ],
        [sds((rows, width), BF16), sds((pairs, LANES, rows), BF16), sds((pairs, 2, rows), F32)],
        [
            pltpu.VMEM((2, 4, half, half), F32),
            pltpu.VMEM((2 * rows, LANES), BF16),
            pltpu.VMEM((2 * rows, 2 * LANES), BF16),
            pltpu.VMEM((4, half, half), F32),
        ],
        prefetch=1,
        cost=cost(4 * rows * 2 * rows * width, 2 * 8 * rows * width, 2 * rows * rows * width // HD),
    )(parity, q, kv, kv, kvo, kvo, qseg, kseg)


def att_bwd_kernel(
    par_ref, q_ref, k_ref, v_ref, ko_ref, vo_ref, g_ref, o_ref, lse_ref, qseg_ref, kseg_ref, c_ref, lo_ref, hi_ref,
    dq_ref, dk_ref, dv_ref, dko_ref, dvo_ref, mask, kpos, vpos, dkpos, dvpos,
):
    rows = q_ref.shape[0]
    half = rows // 2
    parity = par_ref[0]
    lane = lax.broadcasted_iota(jnp.int32, (half, LANES), 1)
    lane_k = lane

    @pl.when(pl.program_id(0) == 0)
    def _():
        for b in range(2):
            quarter = parity if b == 0 else 3 - parity

            def one(j, carry):
                kp = j * half + lax.broadcasted_iota(jnp.int32, (half, half), 0)
                qp = quarter * half + lax.broadcasted_iota(jnp.int32, (half, half), 1)
                same = kseg_ref[pl.ds(pl.multiple_of(j * half, half), half), :] == qseg_ref[b : b + 1, :]
                mask[b, j] = jnp.where((kp <= qp) & same, BIG, NEG)
                return carry

            lax.fori_loop(0, 4, one, 0)

    place_keys(k_ref, ko_ref, kpos, parity)
    place_keys(v_ref, vo_ref, vpos, parity)
    dkpos[...] = jnp.zeros_like(dkpos)
    dvpos[...] = jnp.zeros_like(dvpos)
    scale = HD**-0.5
    for b in range(2):
        quarter = parity if b == 0 else 3 - parity
        at = slice(b * half, (b + 1) * half)
        qs = q_ref[at, :] * jnp.asarray(scale, BF16)
        gs = g_ref[at, :]
        prod = (gs.astype(F32) * o_ref[at, :].astype(F32)).T
        zero = jnp.zeros_like(qs)
        parts = []
        for h in range(2):
            mine = (lane < HD) if h == 0 else (lane >= HD)
            qh = jnp.where(mine, qs, zero)
            gh = jnp.where(mine, gs, zero)
            lse = lse_ref[0, h : h + 1, at]
            delta = jnp.sum(prod[h * HD : (h + 1) * HD, :], axis=0, keepdims=True)

            def tile(j, acc):
                ks = pl.ds(pl.multiple_of(j * half, half), half)
                keys = kpos[ks, :]
                s = jnp.minimum(dot_nt(keys, qh), mask[b, j])
                p = jnp.exp(s - lse)
                dp = dot_nt(vpos[ks, :], gh)
                ds = (p * (dp - delta)).astype(BF16)
                dvpos[ks, :] += dot(p.astype(BF16), gh)
                dkpos[ks, :] += dot(ds, qh)
                return acc + dot(ds, keys, ((0,), (0,)))

            parts.append(lax.fori_loop(0, quarter + 1, tile, jnp.zeros((half, LANES), F32)))
        dq = jnp.where(lane < HD, parts[0], parts[1]) * scale
        dq_ref[at, :] = turn(dq, c_ref[at, :], -lo_ref[at, :], -hi_ref[at, :]).astype(BF16)
    for src, mine, theirs in ((dkpos, dk_ref, dko_ref), (dvpos, dv_ref, dvo_ref)):
        for b in range(2):
            at = slice(b * half, (b + 1) * half)
            own = parity if b == 0 else 3 - parity
            other = 1 - parity if b == 0 else 2 + parity
            mine[at, :] = src[pl.ds(pl.multiple_of(own * half, half), half), :].astype(mine.dtype)
            theirs[at, :] = src[pl.ds(pl.multiple_of(other * half, half), half), :].astype(BF16)


def att_bwd(parity, q, kv, kvo, gob, ob, lse, qseg, kseg, tables):
    rows, width = q.shape
    pairs = width // LANES
    half = rows // 2
    col = lambda off: pl.BlockSpec((rows, LANES), lambda p, r: (0, p + off))
    out = sds((rows, width), F32)
    low = sds((rows, width), BF16)
    return call(
        att_bwd_kernel,
        (pairs,),
        [
            col(0), col(0), col(pairs), col(0), col(pairs), col(0), col(0),
            pl.BlockSpec((1, 2, rows), lambda p, r: (p, 0, 0)),
            whole((2, half)), whole((2 * rows, 1)),
            whole((rows, LANES)), whole((rows, LANES)), whole((rows, LANES)),
        ],
        [col(0)] * 5,
        [low, out, out, low, low],
        [
            pltpu.VMEM((2, 4, half, half), F32),
            pltpu.VMEM((2 * rows, LANES), BF16),
            pltpu.VMEM((2 * rows, LANES), BF16),
            pltpu.VMEM((2 * rows, LANES), F32),
            pltpu.VMEM((2 * rows, LANES), F32),
        ],
        prefetch=1,
        cost=cost(10 * rows * 2 * rows * width, 2 * 16 * rows * width, 2 * rows * rows * width // HD),
    )(parity, q, kv, kv, kvo, kvo, gob, ob, lse, qseg, kseg, *tables)


def up_kernel(n2_ref, w_ref, b_ref, h_ref, dg_ref):
    u_all = dot(n2_ref[...], w_ref[...]) + b_ref[...]
    for g in range(u_all.shape[1] // LANES):
        at = slice(g * LANES, (g + 1) * LANES)
        u = u_all[:, at]
        cdf = 0.5 * (1.0 + lax.erf(u * (1.0 / math.sqrt(2.0))))
        h_ref[:, at] = (u * cdf).astype(BF16)
        pdf = jnp.exp(-0.5 * u * u) * (1.0 / math.sqrt(2.0 * math.pi))
        dg_ref[:, at] = (cdf + u * pdf).astype(BF16)


def up(n2, w, b):
    rows, width = n2.shape
    hidden = w.shape[1]
    cols = 512
    blk = pl.BlockSpec((rows, cols), lambda j: (0, j))
    return call(
        up_kernel,
        (hidden // cols,),
        [whole((rows, width)), pl.BlockSpec((width, cols), lambda j: (0, j)), pl.BlockSpec((1, cols), lambda j: (0, j))],
        [blk, blk],
        [sds((rows, hidden), BF16), sds((rows, hidden), BF16)],
        cost=cost(2 * rows * width * hidden, 2 * (width * hidden + 2 * rows * hidden), 2 * rows * hidden),
    )(n2, w, b)


def out_kernel(ob_ref, hb_ref, wo_ref, wd_ref, bo_ref, bd_ref, x_ref, t_ref, valid_ref, gy_ref, gb_ref, gbt_ref, sum_ref):
    branch = dot(ob_ref[...], wo_ref[...]) + bo_ref[...]
    feed = dot_nt(hb_ref[...], wd_ref[...]) + bd_ref[...]
    y = x_ref[...].astype(F32) + (branch + feed)
    g = valid_ref[...] * (y - t_ref[...].astype(F32))
    low = g.astype(BF16)
    gy_ref[...] = g
    gb_ref[...] = low
    gbt_ref[...] = low.T
    sum_ref[...] = jnp.sum(low.astype(F32), axis=0, keepdims=True)


def out_grad(ob, hb, wo, wd, bo, bd, x, t, valid):
    rows, width = ob.shape
    hidden = hb.shape[1]
    cols = 256
    col = pl.BlockSpec((rows, cols), lambda j: (0, j))
    vec = pl.BlockSpec((1, cols), lambda j: (0, j))
    return call(
        out_kernel,
        (width // cols,),
        [
            whole((rows, width)), whole((rows, hidden)),
            pl.BlockSpec((width, cols), lambda j: (0, j)), pl.BlockSpec((cols, hidden), lambda j: (j, 0)),
            vec, vec, col, col, whole((rows, 1)),
        ],
        [col, col, pl.BlockSpec((cols, rows), lambda j: (j, 0)), vec],
        [sds((rows, width), F32), sds((rows, width), BF16), sds((width, rows), BF16), sds((1, width), F32)],
        cost=cost(2 * rows * width * (width + hidden), 2 * (width * (width + hidden) + 6 * rows * width)),
    )(ob, hb, wo, wd, bo, bd, x, t, valid)


def dgrad_kernel(gb_ref, wo_ref, wd_ref, wu_ref, dg_ref, gob_ref, gub_ref, sum_ref, gn2_ref):
    @pl.when(pl.program_id(0) == 0)
    def _():
        gob_ref[...] = dot_nt(gb_ref[...], wo_ref[...]).astype(BF16)
        gn2_ref[...] = jnp.zeros_like(gn2_ref)

    act = dot(gb_ref[...], wd_ref[...])
    gub = (act * dg_ref[...].astype(F32)).astype(BF16)
    gub_ref[...] = gub
    sum_ref[...] = jnp.sum(gub.astype(F32), axis=0, keepdims=True)
    gn2_ref[...] += dot_nt(gub, wu_ref[...])


def dgrad(gb, wo, wd, wu, dg):
    rows, width = gb.shape
    hidden = dg.shape[1]
    cols = 512
    blk = pl.BlockSpec((rows, cols), lambda j: (0, j))
    wblk = pl.BlockSpec((width, cols), lambda j: (0, j))
    return call(
        dgrad_kernel,
        (hidden // cols,),
        [whole((rows, width)), whole((width, width)), wblk, wblk, blk],
        [whole((rows, width)), blk, pl.BlockSpec((1, cols), lambda j: (0, j)), whole((rows, width))],
        [sds((rows, width), BF16), sds((rows, hidden), BF16), sds((1, hidden), F32), sds((rows, width), F32)],
        cost=cost(2 * rows * width * (width + 2 * hidden), 2 * (width * (width + 2 * hidden) + 6 * rows * width)),
    )(gb, wo, wd, wu, dg)


def last_kernel(
    dq_ref, dk_ref, dv_ref, dko_ref, dvo_ref, c_ref, lo_ref, hi_ref, w_ref, x_ref, vec_ref, gn2_ref, gy_ref,
    gqkv_ref, in_ref, vg_ref, sum_ref, gn1,
):
    j = pl.program_id(0)
    rows, width = x_ref.shape
    cols = w_ref.shape[1]
    nq = width // cols

    @pl.when(j == 0)
    def _():
        gn1[...] = jnp.zeros_like(gn1)

    @pl.when(j < nq)
    def _():
        gqkv_ref[...] = dq_ref[...]

    @pl.when((j >= nq) & (j < 2 * nq))
    def _():
        for g in range(cols // LANES):
            at = slice(g * LANES, (g + 1) * LANES)
            grad = dk_ref[:, at] + dko_ref[:, at].astype(F32)
            gqkv_ref[:, at] = turn(grad, c_ref[...], -lo_ref[...], -hi_ref[...]).astype(BF16)

    @pl.when(j >= 2 * nq)
    def _():
        gqkv_ref[...] = (dv_ref[...] + dvo_ref[...].astype(F32)).astype(BF16)

    low = gqkv_ref[...]
    sum_ref[...] = jnp.sum(low.astype(F32), axis=0, keepdims=True)
    gn1[...] += dot_nt(low, w_ref[...])

    @pl.when(j == 3 * nq - 1)
    def _():
        step = 64
        vg_ref[...] = jnp.zeros_like(vg_ref)

        def chunk(i, carry):
            at = pl.ds(pl.multiple_of(i * step, step), step)
            xh, rstd = normed(x_ref[at, :].astype(F32))
            total = gy_ref[at, :]
            sums = []
            for g_n, gain in ((gn1[at, :], vec_ref[0:1, :]), (gn2_ref[at, :], vec_ref[2:3, :])):
                sums.append(jnp.sum(g_n * xh, axis=0, keepdims=True))
                sums.append(jnp.sum(g_n, axis=0, keepdims=True))
                e = g_n * gain
                mean = jnp.mean(e, axis=-1, keepdims=True)
                along = jnp.mean(e * xh, axis=-1, keepdims=True)
                total = total + rstd * (e - mean - xh * along)
            in_ref[at, :] = total
            vg_ref[...] += jnp.concatenate(sums, axis=0)
            return carry

        lax.fori_loop(0, rows // step, chunk, 0)


def last(dq, dk, dv, dko, dvo, tables, w, x, vec4, gn2, gy):
    rows, width = x.shape
    cols = 512
    nq = width // cols
    at = lambda lo: pl.BlockSpec((rows, cols), lambda j: (0, jnp.clip(j - lo * nq, 0, nq - 1)))
    return call(
        last_kernel,
        (3 * nq,),
        [
            at(0), at(1), at(2), at(1), at(2),
            whole((rows, LANES)), whole((rows, LANES)), whole((rows, LANES)),
            pl.BlockSpec((width, cols), lambda j: (0, j)),
            whole((rows, width)), whole(vec4.shape), whole((rows, width)), whole((rows, width)),
        ],
        [
            pl.BlockSpec((rows, cols), lambda j: (0, j)), whole((rows, width)), whole((4, width)),
            pl.BlockSpec((1, cols), lambda j: (0, j)),
        ],
        [sds((rows, 3 * width), BF16), sds((rows, width), F32), sds((4, width), F32), sds((1, 3 * width), F32)],
        [pltpu.VMEM((rows, width), F32)],
        cost=cost(6 * rows * width * width, 2 * (3 * width * width + 20 * rows * width)),
    )(dq, dk, dv, dko, dvo, *tables, w, x, vec4, gn2, gy)


def update_kernel(f_ref, g_ref, ls_ref, rs_ref, lr_ref, rr_ref, m_ref, nl_ref, nr_ref, nm_ref, mc_ref):
    factor = f_ref[0, 0]
    half_sq = 0.5 * factor * factor
    for k in range(ls_ref.shape[1]):
        at = slice(k * BS, (k + 1) * BS)
        g = g_ref[:, at]
        gt = g.T
        nl_ref[0, k] = 0.5 * ls_ref[0, k] + half_sq * dot(g, gt)
        nr_ref[0, k] = 0.5 * rs_ref[0, k] + half_sq * dot(gt, g)
        tb = (g.astype(F32) * factor).astype(BF16)
        mb = dot(lr_ref[0, k], tb).astype(BF16)
        new = m_ref[:, at] - LEARN * dot(mb, rr_ref[0, k])
        nm_ref[:, at] = new
        mc_ref[:, at] = new.astype(BF16)


def update(factor, g, ls, rs, lr, rr, m):
    rows, total = g.shape
    count = ls.shape[1]
    per = 8
    blk = pl.BlockSpec((1, per, BS, BS), lambda j: (0, j, 0, 0))
    col = pl.BlockSpec((rows, per * BS), lambda j: (0, j))
    return call(
        update_kernel,
        (count // per,),
        [pl.BlockSpec(memory_space=pltpu.SMEM), col, blk, blk, blk, blk, col],
        [blk, blk, col, col],
        [sds(ls.shape, F32), sds(rs.shape, F32), sds(m.shape, F32), sds(m.shape, BF16)],
        cost=cost(8 * rows * total * BS, rows * total * 32),
    )(factor, g, ls, rs, lr, rr, m)


PAIR = 1024
TILE = PAIR // 2


def bits_of(index, count):
    return [(index // (1 << b)) % 2 for b in range(count)]


def reduce_kernel(plan, levels, replica_bits, *refs):
    groups = len(plan)
    pairs = sum(plan)
    at_refs, b_refs = refs[:groups], refs[groups : 2 * groups]
    v_ref, g_out, vec_out, sq_out = refs[2 * groups : 2 * groups + 4]
    (a_own, a_oth, b_own, b_oth, s1, r1, r2, zs, gs, vr, vd, sq, sq_in,
     sem_l, sem_b, sem_as, sem_ar, sem_bs, sem_br, sem_1s, sem_1r, sem_2s, sem_2r,
     sem_zs, sem_zr, sem_gs, sem_gr, sem_vs, sem_vr, sem_qs, sem_qr, sem_o) = refs[2 * groups + 4 :]
    s = lax.axis_index("shard")
    z = lax.axis_index("dp")
    core, x, y = bits_of(s, 3)
    zb = bits_of(z, replica_bits)
    to_core = {"shard": s + 1 - 2 * core}
    to_x = {"shard": s + 2 - 4 * x}
    to_y = {"shard": s + 4 - 8 * y}
    to_z = [{"dp": z + (1 - 2 * zb[l]) * (1 << l)} for l in range(replica_bits)]
    peers = [to_core, to_x, to_y] + to_z

    barrier = pltpu.get_barrier_semaphore()
    for peer in peers:
        pl.semaphore_signal(barrier, inc=1, device_id=peer, device_id_type=pl.DeviceIdType.MESH)
    pl.semaphore_wait(barrier, len(peers))

    def remote(src, dst, send, recv, peer):
        return pltpu.make_async_remote_copy(
            src_ref=src, dst_ref=dst, send_sem=send, recv_sem=recv, device_id=peer, device_id_type=pl.DeviceIdType.MESH
        )

    first = [sum(plan[:w]) for w in range(groups + 1)]

    def a_local(w):
        return pltpu.make_async_copy(at_refs[w].at[:, core], a_own.at[w], sem_l.at[w])

    def a_send(w):
        return remote(at_refs[w].at[:, 1 - core], a_oth.at[w], sem_as.at[w], sem_ar.at[w], to_core)

    def b_cols(w, i):
        return b_refs[w].at[:, pl.ds(pl.multiple_of((i - first[w]) * PAIR, PAIR), PAIR)]

    def b_send(w, i):
        return remote(b_cols(w, i), b_oth.at[i], sem_bs.at[i], sem_br.at[i], to_core)

    def b_local(w, i):
        return pltpu.make_async_copy(b_cols(w, i), b_own.at[i % 2], sem_b.at[i % 2])

    for w in range(groups):
        a_local(w).start()
        a_send(w).start()
        if w == 0:
            b_local(0, 0).start()

        def launch(i, carry, w=w):
            b_send(w, i).start()
            return carry

        lax.fori_loop(first[w], first[w + 1], launch, 0)

    v4 = v_ref
    vecs = [
        (v4.at[:, :, 1 - core], vr.at[0, :, :], to_core),
        (vr.at[0, :, 1 - x], vr.at[1, 0, :], to_x),
        (vr.at[1, 0, 1 - y], vr.at[1, 1, 0], to_y),
    ]

    def v_copy(k):
        if k < 3:
            src, dst, peer = vecs[k]
        else:
            src, dst, peer = vd.at[2 * (k - 3)], vd.at[2 * (k - 3) + 1], to_z[k - 3]
        return remote(src, dst, sem_vs.at[k], sem_vr.at[k], peer)

    def v_done(k):
        v_copy(k).wait()
        if k == 0:
            vr[0] = vr[0] + v4[:, :, core]
        elif k == 1:
            vr[1, 0] = vr[1, 0] + vr[0, :, x]
        else:
            if k == 2:
                total = vr[1, 1, 0] + vr[1, 0, y]
            else:
                total = vd[2 * (k - 3)] + vd[2 * (k - 3) + 1]
            vd[2 * (k - 2)] = total

    v_hops = 3 + replica_bits
    v_copy(0).start()
    sq[...] = jnp.zeros_like(sq)

    def copy1(i, t):
        src = s1.at[i, t, :, 1 - x] if t == 0 else s1.at[i, t, 1 - y]
        return remote(src, r1.at[i, t], sem_1s.at[i, t], sem_1r.at[i, t], to_x if t == 0 else to_y)

    def copy2(i, t):
        bit = y if t == 0 else x
        return remote(
            r1.at[i, t, 1 - bit], r2.at[i, :, t * TILE : (t + 1) * TILE],
            sem_2s.at[i, t], sem_2r.at[i, t], to_y if t == 0 else to_x,
        )

    starts = [0]
    for l in range(levels):
        starts.append(starts[l] + (BS >> (l + 1)))

    def z_rows(l):
        return pl.ds(starts[l], BS >> (l + 1))

    def level_src(i, l, half):
        size = BS >> (l + 1)
        off = pl.multiple_of(half * size, size)
        if l == 0:
            return r2.at[i, pl.ds(off, size)]
        return zs.at[i, pl.ds(pl.multiple_of(starts[l - 1] + off, size), size)]

    def copy_z(i, l):
        return remote(
            level_src(i, l, 1 - zb[l]), zs.at[i, z_rows(l)], sem_zs.at[i, l], sem_zr.at[i, l], to_z[l]
        )

    def g_rows(l, mine):
        base = sum((zb[m] * (BS >> (m + 1)) for m in range(l)), 0)
        size = BS >> (l + 1)
        half = zb[l] if mine else 1 - zb[l]
        return pl.ds(pl.multiple_of(base + half * size, size), size)

    def copy_g(i, l):
        return remote(gs.at[i, g_rows(l, True)], gs.at[i, g_rows(l, True)], sem_gs.at[i, l], sem_gr.at[i, l], to_z[l])

    def out_cols(i):
        total = g_out.shape[1] // PAIR
        spot = total - first[1] + i
        spot = jnp.where(i >= first[1], i - first[1] + plan[3], spot)
        spot = jnp.where(i >= first[3], i - first[3], spot)
        return pl.ds(pl.multiple_of(spot * PAIR, PAIR), PAIR)

    def out_copy(i):
        src = gs.at[i] if levels else r2.at[i]
        return pltpu.make_async_copy(src, g_out.at[:, out_cols(i)], sem_o.at[i])

    def stage_a(i):
        group = sum((jnp.where(i >= first[w], 1, 0) for w in range(1, groups)), 0)
        for w in range(groups):
            @pl.when(i == first[w])
            def _():
                a_local(w).wait()
                a_send(w).wait()

            @pl.when((i + 1 >= first[w]) & (i + 1 < first[w + 1]))
            def _():
                b_local(w, i + 1).start()

        slot = i % 2
        pltpu.make_async_copy(b_oth.at[i], b_own.at[slot], sem_b.at[slot]).wait()
        remote(b_own.at[slot], b_oth.at[i], sem_bs.at[i], sem_br.at[i], to_core).wait()
        size = 4 * BS
        own = a_own[group].reshape(size, a_own.shape[-1])
        oth = a_oth[group].reshape(size, a_oth.shape[-1])
        for t in range(2):
            at = slice(t * TILE, (t + 1) * TILE)
            acc = dot(own, b_own[slot, :, at]) + dot(oth, b_oth[i, :, at])
            s1[i, t] = acc.astype(BF16).reshape(2, 2, BS, TILE)
            copy1(i, t).start()

    def stage_b(i):
        for t in range(2):
            copy1(i, t).wait()
            kept = s1[i, t, :, x] if t == 0 else s1[i, t, y]
            r1[i, t] = (r1[i, t].astype(F32) + kept.astype(F32)).astype(BF16)
            copy2(i, t).start()

    def stage_c(i):
        for t in range(2):
            copy2(i, t).wait()
            at = slice(t * TILE, (t + 1) * TILE)
            bit = y if t == 0 else x
            r2[i, :, at] = (r2[i, :, at].astype(F32) + r1[i, t, bit].astype(F32)).astype(BF16)
        if levels:
            copy_z(i, 0).start()
        else:
            out_copy(i).start()

    def stage_z(l):
        def run(i):
            copy_z(i, l).wait()
            total = zs[i, z_rows(l)].astype(F32) + level_src(i, l, zb[l])[...].astype(F32)
            if l + 1 < levels:
                zs[i, z_rows(l)] = total.astype(BF16)
                copy_z(i, l + 1).start()
            else:
                gs[i, g_rows(l, True)] = total.astype(BF16)
                copy_g(i, l).start()
        return run

    def stage_g(l):
        def run(i):
            copy_g(i, l).wait()
            if l:
                copy_g(i, l - 1).start()
            else:
                part = gs[i].astype(F32)
                part = jnp.sum((part * part).reshape(BS // 8, 8, PAIR), axis=0)
                sq[0] += sum(part[:, g * LANES : (g + 1) * LANES] for g in range(PAIR // LANES))
                out_copy(i).start()
        return run

    stages = [stage_a, stage_b, stage_c]
    stages += [stage_z(l) for l in range(levels)] + [stage_g(l) for l in reversed(range(levels))]
    lags = len(stages)

    def step(i, carry):
        for lag, stage in enumerate(stages):
            @pl.when((i >= lag) & (i < pairs + lag))
            def _():
                stage(i - lag)

        for k in range(v_hops):
            @pl.when(i == k + 1)
            def _():
                v_done(k)
                if k + 1 < v_hops:
                    v_copy(k + 1).start()
        return carry

    lax.fori_loop(0, pairs + lags - 1, step, 0)
    total = vd[2 * replica_bits]
    vec_out[...] = total
    rows13 = lax.broadcasted_iota(jnp.int32, total.shape, 0) < 13
    square = jnp.where(rows13, total * total, 0.0)
    sq[0] += square[0:8] + square[8:16]
    for k, peer in enumerate((to_core, to_x, to_y)):
        hop = remote(sq.at[k], sq_in.at[k], sem_qs.at[k], sem_qr.at[k], peer)
        hop.start()
        hop.wait()
        sq[k + 1] = sq[k] + sq_in[k]
    sq_out[...] = sq[3]

    def drain(i, carry):
        out_copy(i).wait()
        return carry

    lax.fori_loop(0, pairs, drain, 0)


def reduce_grads(ats, bs, vec, replicas):
    plan = [b.shape[1] // PAIR for b in bs]
    pairs = sum(plan)
    tokens = bs[0].shape[0]
    replica_bits = replicas.bit_length() - 1
    assert replicas == 1 << replica_bits
    levels = replica_bits if replicas <= 8 else 0
    groups = len(plan)
    dma = pltpu.SemaphoreType.DMA
    lv, vh = max(levels, 1), 3 + replica_bits
    scratch = [
        pltpu.VMEM((groups, 4, BS, tokens), BF16),
        pltpu.VMEM((groups, 4, BS, tokens), BF16),
        pltpu.VMEM((2, tokens, PAIR), BF16),
        pltpu.VMEM((pairs, tokens, PAIR), BF16),
        pltpu.VMEM((pairs, 2, 2, 2, BS, TILE), BF16),
        pltpu.VMEM((pairs, 2, 2, BS, TILE), BF16),
        pltpu.VMEM((pairs, BS, PAIR), BF16),
        pltpu.VMEM((pairs, BS if levels else 16, PAIR), BF16),
        pltpu.VMEM((pairs if levels else 1, BS, PAIR), BF16),
        pltpu.VMEM((2, 2, 2, 16, LANES), F32),
        pltpu.VMEM((2 * replica_bits + 2, 16, LANES), F32),
        pltpu.VMEM((4, 8, LANES), F32),
        pltpu.VMEM((3, 8, LANES), F32),
        dma((groups,)), dma((2,)), dma((groups,)), dma((groups,)), dma((pairs,)), dma((pairs,)),
        dma((pairs, 2)), dma((pairs, 2)), dma((pairs, 2)), dma((pairs, 2)),
        dma((pairs, lv)), dma((pairs, lv)), dma((pairs, lv)), dma((pairs, lv)),
        dma((vh,)), dma((vh,)), dma((3,)), dma((3,)), dma((pairs,)),
    ]
    anyspace = pl.BlockSpec(memory_space=pl.ANY)
    vmem = pl.BlockSpec(memory_space=pltpu.VMEM)
    return pl.pallas_call(
        partial(reduce_kernel, plan, levels, replica_bits),
        out_shape=[
            sds((BS, pairs * PAIR), BF16), sds((16, LANES), F32), sds((8, LANES), F32)
        ],
        in_specs=[anyspace] * (2 * groups) + [vmem],
        out_specs=[anyspace, vmem, vmem],
        scratch_shapes=scratch,
        compiler_params=pltpu.CompilerParams(
            collective_id=0, has_side_effects=True, vmem_limit_bytes=58 * MIB
        ),
    )(*[a.reshape(4, 2, BS, tokens) for a in ats], *bs, vec)


def angles(positions):
    half_rot = ROT // 2
    frequency = jnp.power(10000.0, -2.0 * jnp.arange(half_rot, dtype=F32) / ROT)
    grid = positions.astype(F32)[:, None] * frequency[None, :]
    cosine, sine = jnp.cos(grid), jnp.sin(grid)
    rows = positions.shape[0]
    ones = jnp.ones((rows, HD - ROT), F32)
    zero = jnp.zeros((rows, HD - ROT), F32)
    blank = jnp.zeros((rows, half_rot), F32)
    c = jnp.concatenate([cosine, cosine, ones] * 2, axis=1)
    lo = jnp.concatenate([-sine, blank, zero] * 2, axis=1)
    hi = jnp.concatenate([blank, sine, zero] * 2, axis=1)
    return c, lo, hi


def body(
    tokens, targets, segments, valid, master, vectors, left_stat, right_stat, left_root, right_root, vector_stat,
):
    rows, width = tokens.shape
    stack = master.shape[1]
    hidden = (stack - 4 * width) // 2
    half = rows // 2
    shards = lax.axis_size("shard")
    replicas = lax.axis_size("dp")
    index = lax.axis_index("shard")
    parity = index % 2
    par = parity.astype(jnp.int32).reshape(1)
    swap = [(i, i ^ 1) for i in range(shards)]

    low = master.astype(BF16)
    w_qkv = lax.all_gather(low[:, : 3 * width], "shard", axis=0, tiled=True)
    w_rest = lax.all_gather(low[:, 3 * width :], "shard", axis=0, tiled=True)
    params = lax.all_gather(vectors.astype(BF16), "shard", axis=0, tiled=True).astype(F32)
    w_out = w_rest[:, :width]
    w_up = w_rest[:, width : width + hidden]
    w_down = w_rest[:, width + hidden :]

    vec4 = params[: 4 * width].reshape(4, width)
    b_qkv = params[4 * width : 7 * width].reshape(1, -1)
    b_out = params[7 * width : 8 * width].reshape(1, -1)
    b_up = params[8 * width : 8 * width + hidden].reshape(1, -1)
    b_down = params[8 * width + hidden :].reshape(1, -1)

    valid_float = valid.astype(F32)

    local = jnp.arange(half, dtype=jnp.int32)
    positions = jnp.concatenate([parity * half + local, (3 - parity) * half + local])
    tables = angles(positions)
    start = (index - parity) * rows
    sequence = lax.dynamic_slice_in_dim(segments, start, 2 * rows).reshape(4, half)
    key_seg = jnp.stack([sequence[0], sequence[2], sequence[3], sequence[1]])
    own_seg = lax.dynamic_slice_in_dim(segments, index * rows, rows)

    n1t, n2, n2t, q, kv = pre(tokens, vec4, w_qkv, b_qkv, tables)
    kvo = lax.ppermute(kv, "shard", swap)
    hb, dg = up(n2, w_up, b_up)
    ob, obt, lse = att_fwd(par, q, kv, kvo, own_seg.reshape(rows, 1), key_seg)
    obt = obt.reshape(width, rows)
    gy, gb, gbt, gb_sum = out_grad(
        ob, hb, w_out, w_down, b_out, b_down, tokens, targets, valid_float.reshape(rows, 1)
    )
    gob, gub, gub_sum, gn2 = dgrad(gb, w_out, w_down, w_up, dg)

    dq, dk, dv, dk_o, dv_o = att_bwd(
        par, q, kv, kvo, gob, ob, lse, own_seg.reshape(2, half), key_seg.reshape(2 * rows, 1), tables
    )
    dk_r = lax.ppermute(dk_o, "shard", swap)
    dv_r = lax.ppermute(dv_o, "shard", swap)
    gqkv, input_grad, vec_grad, gqkv_sum = last(
        dq, dk, dv, dk_r, dv_r, tables, w_qkv, tokens, vec4, gn2, gy
    )
    own_len = vectors.shape[0]
    lines = own_len // LANES
    vector_grad = jnp.concatenate(
        [vec_grad.reshape(-1), gqkv_sum.reshape(-1), gb_sum.reshape(-1), gub_sum.reshape(-1), gb_sum.reshape(-1)]
    ).reshape(shards, lines, LANES)
    tail = jnp.full((shards, 16 - lines, LANES), jnp.sum(valid.astype(F32)), F32)
    packed = jnp.concatenate([vector_grad, tail], axis=1).reshape(2, 2, 2, 16, LANES)
    grads, vec_total, squares = reduce_grads((gbt, obt, n2t, n1t), (hb, gb, gub, gqkv), packed, replicas)
    own_vector = vec_total[:lines].reshape(own_len)
    scale = rows * shards * replicas / vec_total[lines, 0]
    if replicas <= 8:
        square_sum = jnp.sum(squares)
    else:
        grads = lax.psum_scatter(grads, "dp", scatter_dimension=1, tiled=True)
        grads = lax.all_gather(grads, "dp", axis=1, tiled=True)
        square_sum = jnp.sum(squares) + lax.psum(jnp.sum(jnp.square(grads.astype(F32))), "shard")
    input_grad = input_grad * scale
    grad_norm = scale * jnp.sqrt(square_sum)
    factor = scale * jnp.minimum(1.0, math.sqrt(width * stack / BS) / grad_norm)
    new_left, new_right, new_master, master_copy = update(
        factor.reshape(1, 1), grads, left_stat, right_stat, left_root, right_root, master
    )
    scaled_vec = own_vector * factor
    new_vstat = 0.5 * vector_stat + 0.5 * scaled_vec * scaled_vec
    new_vectors = vectors - LEARN_VEC * scaled_vec / jnp.sqrt(new_vstat)
    return (input_grad, grad_norm, new_left, new_right, new_master, master_copy, new_vectors, new_vstat)


def solution(mesh):
    rows = P(("dp", "shard"), None)
    quad = P("shard", None, None, None)
    return jax.shard_map(
        body,
        mesh=mesh,
        in_specs=(
            rows, rows, P("dp"), P(("dp", "shard")), P("shard", None), P("shard"), quad, quad, quad, quad, P("shard"),
        ),
        out_specs=(rows, P(), quad, quad, P("shard", None), P("shard", None), P("shard"), P("shard")),
        check_vma=False,
    )
```

```python
from functools import partial
import math

import jax
import jax.numpy as jnp
from jax import lax
from jax.experimental import pallas as pl
from jax.experimental.pallas import tpu as pltpu
from jax.sharding import PartitionSpec as P

HD = 64
ROT = 16
BS = 128
LANES = 128
EPS = 1e-05
NEG = -1e30
BIG = 3e38
LEARN = 0.5
LEARN_VEC = 0.15
F32 = jnp.float32
BF16 = jnp.bfloat16
MIB = 1 << 20


def dot(a, b, dims=((1,), (0,))):
    return lax.dot_general(a, b, (dims, ((), ())), preferred_element_type=F32)


def dot_nt(a, b):
    return dot(a, b, ((1,), (1,)))


def call(kernel, grid, in_specs, out_specs, out_shape, scratch=(), vmem=48, prefetch=0, cost=None):
    return pl.pallas_call(
        kernel,
        out_shape=out_shape,
        grid_spec=pltpu.PrefetchScalarGridSpec(
            num_scalar_prefetch=prefetch,
            grid=grid,
            in_specs=in_specs,
            out_specs=out_specs,
            scratch_shapes=list(scratch),
        ),
        compiler_params=pltpu.CompilerParams(
            vmem_limit_bytes=vmem * MIB, dimension_semantics=("arbitrary",) * len(grid)
        ),
        cost_estimate=cost,
    )


def cost(flops, nbytes, trans=0):
    return pl.CostEstimate(flops=int(flops), bytes_accessed=int(nbytes), transcendentals=int(trans))


def whole(shape):
    rank = len(shape)
    return pl.BlockSpec(shape, lambda *g: (0,) * rank)


def sds(shape, dtype):
    return jax.ShapeDtypeStruct(shape, dtype)


def normed(x):
    mean = jnp.mean(x, axis=-1, keepdims=True)
    centred = x - mean
    rstd = lax.rsqrt(jnp.mean(centred * centred, axis=-1, keepdims=True) + EPS)
    return centred * rstd, rstd


def turn(values, c, lo, hi):
    return values * c + pltpu.roll(values, LANES - ROT // 2, 1) * lo + pltpu.roll(values, ROT // 2, 1) * hi


def place_keys(own_ref, other_ref, out_ref, parity):
    half = own_ref.shape[0] // 2
    for ref, who in ((own_ref, parity), (other_ref, 1 - parity)):
        for b in range(2):
            quarter = who if b == 0 else 3 - who
            out_ref[pl.ds(pl.multiple_of(quarter * half, half), half), :] = ref[b * half : (b + 1) * half, :]


def key_tile(t, parity):
    first = parity + 1
    b = jnp.where(t >= first, 1, 0)
    return b, t - b * first


def split_heads(pair):
    lane = lax.broadcasted_iota(jnp.int32, pair.shape, 1)
    zero = jnp.zeros_like(pair)
    return jnp.concatenate([jnp.where(lane < HD, pair, zero), jnp.where(lane >= HD, pair, zero)], axis=0)


def join_heads(both):
    half = both.shape[0] // 2
    lane = lax.broadcasted_iota(jnp.int32, (half, LANES), 1)
    return jnp.where(lane < HD, both[:half], both[half:])


CHUNK = 1024


def bits_of(index, count):
    return [(index // (1 << b)) % 2 for b in range(count)]


def flipped(bits, mask):
    return sum(((1 - bit) if (mask >> k) & 1 else bit) * (1 << k) for k, bit in enumerate(bits))


def remote(src, dst, send, recv, peer):
    return pltpu.make_async_remote_copy(
        src_ref=src, dst_ref=dst, send_sem=send, recv_sem=recv, device_id=peer, device_id_type=pl.DeviceIdType.MESH
    )


def meet(peers):
    barrier = pltpu.get_barrier_semaphore()
    for peer in peers:
        pl.semaphore_signal(barrier, inc=1, device_id=peer, device_id_type=pl.DeviceIdType.MESH)
    pl.semaphore_wait(barrier, len(peers))


def column(row):
    return jnp.broadcast_to(row.astype(F32), (LANES, row.shape[1])).T


def rotary_tables(parity, rows, c_ref, lo_ref, hi_ref):
    half = rows // 2
    lane = lax.broadcasted_iota(jnp.int32, (1, LANES), 1) % HD
    frequency = jnp.zeros((1, LANES), F32)
    for k in range(ROT // 2):
        value = 10000.0 ** (-2.0 * k / ROT)
        frequency = jnp.where((lane < ROT) & (lane % (ROT // 2) == k), value, frequency)
    step = 64

    def chunk(i, carry):
        row = i * step + lax.broadcasted_iota(jnp.int32, (step, LANES), 0)
        late = (i * step) // half
        quarter = parity + late * (3 - 2 * parity)
        position = (row - late * half + quarter * half).astype(F32)
        grid = position * frequency
        at = pl.ds(pl.multiple_of(i * step, step), step)
        sine = jnp.sin(grid)
        c_ref[at, :] = jnp.cos(grid)
        lo_ref[at, :] = jnp.where(lane < ROT // 2, -sine, 0.0)
        hi_ref[at, :] = jnp.where((lane >= ROT // 2) & (lane < ROT), sine, 0.0)
        return carry

    lax.fori_loop(0, rows // step, chunk, 0)


def fwd_kernel(
    total, replica_bits,
    m_ref, v_ref, x_ref, t_ref, valid_ref, seg_ref,
    w_out, n1t_out, n2t_out, obt_out, gbt_out, q_out, kv_out, kvo_out, ob_out, hb_out, dg_out, gy_out, gb_out, tab_out,
    lse_ref, sum_ref, par_ref, scale_ref,
    w, stage, vbuf, n1, n2, n1t, n2t, qkv, kvo, hb, dg, ob, fy, sc, top, acc, mask, kpos, vpos, tab, cnt, cnt_in,
    sem_m, sem_w, sem_s, sem_r, sem_vs, sem_vr, sem_ks, sem_kr, sem_cs, sem_cr, sem_o,
):
    rows, width = x_ref.shape
    half = rows // 2
    stack = m_ref.shape[1]
    chunks = stack // CHUNK
    hidden = (stack - 4 * width) // 2
    per = hidden // CHUNK
    s = lax.axis_index("shard")
    z = lax.axis_index("dp")
    sb = bits_of(s, 3)
    zb = bits_of(z, replica_bits)
    core, x, y = sb
    parity = core
    to = [{"shard": flipped(sb, k)} for k in range(8)]
    to_z = [{"dp": z + (1 - 2 * zb[l]) * (1 << l)} for l in range(replica_bits)]
    blk = [flipped(sb, k) for k in range(8)]
    CORE, XX, YY = 1, 2, 4

    def load(c):
        return pltpu.make_async_copy(m_ref.at[:, c * CHUNK : (c + 1) * CHUNK], stage.at[c % 3], sem_m.at[c % 3])

    for c in range(3):
        load(c).start()
    meet(to[1:] + to_z)

    vbuf[pl.ds(s, 1)] = v_ref[...].reshape(1, 16, LANES)
    v_sends = [remote(v_ref, vbuf.at[s], sem_vs.at[k - 1], sem_vr.at[k - 1], to[k]) for k in range(1, 8)]
    for copy in v_sends:
        copy.start()

    def cols(c):
        return pl.ds(pl.multiple_of(c * CHUNK, CHUNK), CHUNK)

    def copy(kind, c):
        at = cols(c)
        top_half, low_half = pl.ds(0, BS // 2), pl.ds(BS // 2, BS // 2)
        if kind < 3:
            ref, peer = w.at[s, :, at], to[(XX, YY, CORE)[kind]]
        elif kind == 3:
            ref, peer = w.at[blk[XX], top_half, at], to[YY]
        elif kind == 4:
            ref, peer = w.at[blk[YY], low_half, at], to[XX]
        else:
            ref, peer = w.at[blk[(XX, YY, XX + YY)[kind - 5]], :, at], to[CORE]
        return remote(ref, ref, sem_s.at[kind, c], sem_r.at[kind, c], peer)

    def send(c):
        for kind in range(3):
            copy(kind, c).start()

    def forward(c):
        copy(0, c).wait()
        copy(1, c).wait()
        for kind in (3, 4, 5, 6):
            copy(kind, c).start()

    def corner(c):
        copy(3, c).wait()
        copy(4, c).wait()
        copy(7, c).start()

    def w_copy(c):
        return pltpu.make_async_copy(w.at[:, :, cols(c)], w_out.at[:, :, cols(c)], sem_w.at[c])

    def finish(c):
        for kind in (2, 5, 6, 7):
            copy(kind, c).wait()
        w_copy(c).start()

    for c in range(chunks):
        load(c).wait()
        w[pl.ds(s, 1), :, c * CHUNK : (c + 1) * CHUNK] = stage[c % 3].astype(BF16).reshape(1, BS, CHUNK)
        if c + 3 < chunks:
            load(c + 3).start()
        if c < 2:
            send(c)

    def hop(k):
        return remote(cnt.at[k], cnt_in.at[k], sem_cs.at[k], sem_cr.at[k], ([to[1], to[2], to[4]] + to_z)[k])

    hops = 3 + replica_bits
    cnt[0] = jnp.full((8, LANES), jnp.sum(valid_ref[...]), F32)
    hop(0).start()

    rotary_tables(parity, rows, tab.at[0], tab.at[1], tab.at[2])
    for copy_v in v_sends:
        copy_v.wait()
    lines = total // (8 * LANES)
    for k in range(8):
        block = vbuf[k].astype(BF16).astype(F32)
        for r in range(lines):
            flat = (k * lines + r) * LANES
            par_ref[0:1, flat : flat + LANES] = block[r : r + 1, :]

    def param(start, size):
        return par_ref[0:1, start : start + size]

    step = 128

    def norms(i, carry):
        at = pl.ds(pl.multiple_of(i * step, step), step)
        xh, _ = normed(x_ref[at, :].astype(F32))
        one = (xh * param(0, width) + param(width, width)).astype(BF16)
        two = (xh * param(2 * width, width) + param(3 * width, width)).astype(BF16)
        n1[at, :] = one
        n2[at, :] = two
        for b in range(width // BS):
            n1t[b, :, at] = one[:, b * BS : (b + 1) * BS].T
            n2t[b, :, at] = two[:, b * BS : (b + 1) * BS].T
        return carry

    lax.fori_loop(0, rows // step, norms, 0)

    def out(k, src, dst):
        return pltpu.make_async_copy(src, dst, sem_o.at[k])

    writes = [
        out(0, n1t, n1t_out), out(1, n2t, n2t_out), out(2, tab, tab_out), out(3, qkv.at[0], q_out),
        out(4, qkv.at[pl.ds(1, 2)], kv_out), out(5, kvo, kvo_out), out(6, ob, ob_out), out(7, hb, hb_out),
        out(8, dg, dg_out), out(9, n2t, obt_out), out(10, n1t, gbt_out), out(11, n1, gb_out), out(12, fy, gy_out),
    ]
    for k in range(3):
        writes[k].start()

    first_row = 4 * (s // 2)

    def see(t, carry):
        b, j = key_tile(t, parity)
        quarter = jnp.where(b == 0, parity, 3 - parity)
        qrow = first_row + 2 * parity + b
        krow = first_row + jnp.where(j == 0, 0, jnp.where(j == 3, 1, j + 1))
        qseg = column(seg_ref[qrow])
        for g in range(half // LANES):
            kseg = seg_ref[krow][:, g * LANES : (g + 1) * LANES].astype(F32)
            qpos = quarter * half + lax.broadcasted_iota(jnp.int32, (half, LANES), 0)
            kp = j * half + g * LANES + lax.broadcasted_iota(jnp.int32, (half, LANES), 1)
            mask[t, :, g * LANES : (g + 1) * LANES] = jnp.where((kp <= qpos) & (qseg == kseg), BIG, NEG)
        return carry

    lax.fori_loop(0, 5, see, 0)
    for j in range(4):
        vpos[j * half : (j + 1) * half, LANES:] = jnp.ones((half, LANES), BF16)

    def kv_send(m):
        return remote(qkv.at[m], kvo.at[m - 1], sem_ks.at[m - 1], sem_kr.at[m - 1], to[CORE])

    sub = 512

    def project(m):
        def part(i, carry):
            off = pl.multiple_of(m * CHUNK + i * sub, sub)
            wide = w[:, :, pl.ds(off, sub)].reshape(width, sub)
            proj = dot(n1[...], wide) + par_ref[0:1, pl.ds(pl.multiple_of(4 * width + off, sub), sub)]
            turned = m < 2
            for g in range(sub // LANES):
                piece = proj[:, g * LANES : (g + 1) * LANES]
                piece = jnp.where(turned, turn(piece, tab[0], tab[1], tab[2]), piece)
                qkv[m, :, pl.ds(pl.multiple_of(i * sub + g * LANES, LANES), LANES)] = piece.astype(BF16)
            return carry

        lax.fori_loop(0, CHUNK // sub, part, 0)

    def upward(k):
        def part(i, carry):
            off = pl.multiple_of(k * CHUNK + i * sub, sub)
            wide = w[:, :, pl.ds(pl.multiple_of(4 * width + off, sub), sub)].reshape(width, sub)
            bias = par_ref[0:1, pl.ds(pl.multiple_of(8 * width + off, sub), sub)]
            wide_u = dot(n2[...], wide) + bias
            for g in range(sub // LANES):
                u = wide_u[:, g * LANES : (g + 1) * LANES]
                cdf = 0.5 * (1.0 + lax.erf(u * (1.0 / math.sqrt(2.0))))
                pdf = jnp.exp(-0.5 * u * u) * (1.0 / math.sqrt(2.0 * math.pi))
                at = pl.ds(pl.multiple_of(off + g * LANES, LANES), LANES)
                hb[:, at] = (u * cdf).astype(BF16)
                dg[:, at] = (cdf + u * pdf).astype(BF16)
            return carry

        lax.fori_loop(0, CHUNK // sub, part, 0)

    def branch():
        def part(i, carry):
            at = pl.ds(pl.multiple_of(i * sub, sub), sub)
            wide = w[:, :, pl.ds(pl.multiple_of(3 * width + i * sub, sub), sub)].reshape(width, sub)
            bias = par_ref[0:1, pl.ds(pl.multiple_of(7 * width + i * sub, sub), sub)]
            fy[:, at] = dot(ob[...], wide) + bias
            return carry

        lax.fori_loop(0, width // sub, part, 0)

    def feed(k):
        def part(i, carry):
            at = pl.ds(pl.multiple_of(i * sub, sub), sub)
            off = pl.ds(pl.multiple_of(4 * width + hidden + k * CHUNK, CHUNK), CHUNK)
            tall = w[pl.ds(i * (sub // BS), sub // BS), :, off].reshape(sub, CHUNK)
            fy[:, at] += dot_nt(hb[:, pl.ds(pl.multiple_of(k * CHUNK, CHUNK), CHUNK)], tall)
            return carry

        lax.fori_loop(0, width // sub, part, 0)

    scale = jnp.asarray(HD**-0.5, BF16)

    def attend(p):
        lanes = pl.ds(pl.multiple_of(p * LANES, LANES), LANES)
        place_keys(qkv.at[1, :, lanes], kvo.at[0, :, lanes], kpos, parity)
        place_keys(qkv.at[2, :, lanes], kvo.at[1, :, lanes], vpos.at[:, 0:LANES], parity)
        top[...] = jnp.full_like(top, NEG)
        acc[...] = jnp.zeros_like(acc)

        def score(t, carry):
            b, j = key_tile(t, parity)
            both = split_heads(qkv[0, pl.ds(pl.multiple_of(b * half, half), half), lanes] * scale)
            keys = kpos[pl.ds(pl.multiple_of(j * half, half), half), :]
            got = dot_nt(both, keys)
            m = mask[t]
            got = jnp.concatenate([jnp.minimum(got[:half], m), jnp.minimum(got[half:], m)], axis=0)
            sc[t] = got
            best = top[b]
            for g in range(half // LANES):
                best = jnp.maximum(best, got[:, g * LANES : (g + 1) * LANES])
            top[b] = best
            return carry

        lax.fori_loop(0, 5, score, 0)
        for b in range(2):
            top[b] = jnp.broadcast_to(jnp.max(top[b], axis=1, keepdims=True), top.shape[1:])

        def weigh(t, carry):
            b, j = key_tile(t, parity)
            best = top[b]
            prob = jnp.exp(sc[t] - jnp.concatenate([best] * (half // LANES), axis=1)).astype(BF16)
            acc[b] += dot(prob, vpos[pl.ds(pl.multiple_of(j * half, half), half), :])
            return carry

        lax.fori_loop(0, 5, weigh, 0)
        for b in range(2):
            at = slice(b * half, (b + 1) * half)
            den = acc[b, :, LANES:]
            lse = (top[b] + jnp.log(den)).T[0:1, :]
            lse_ref[p, 0:1, at] = lse[:, :half]
            lse_ref[p, 1:2, at] = lse[:, half:]
            got = join_heads(acc[b, :, :LANES] / den).astype(BF16)
            ob[at, lanes] = got
            n2t[p, :, at] = got.T

    pairs = width // LANES
    first_att = 6
    each = 2

    def tick(k, carry):
        @pl.when(k < chunks)
        def _():
            forward(k)

        @pl.when(k + 2 < chunks)
        def _():
            send(k + 2)

        @pl.when((k >= 1) & (k - 1 < chunks))
        def _():
            corner(k - 1)

        done = k - 2

        @pl.when(done >= 0)
        def _():
            finish(done)

        for h in range(hops):
            @pl.when(k == h + 1)
            def _():
                hop(h).wait()
                cnt[h + 1] = cnt[h] + cnt_in[h]
                if h + 1 < hops:
                    hop(h + 1).start()

        @pl.when((done >= 0) & (done < 3))
        def _():
            project(done)

        for m in (1, 2):
            @pl.when(done == m)
            def _():
                kv_send(m).start()

        @pl.when((done >= 4) & (done < 4 + per))
        def _():
            upward(done - 4)

        @pl.when(k == first_att)
        def _():
            for m in (1, 2):
                kv_send(m).wait()
            writes[3].start()
            writes[4].start()
            writes[5].start()
            writes[1].wait()

        @pl.when((k >= first_att) & (k < first_att + pairs // each))
        def _():
            def pair(i, carry):
                attend((k - first_att) * each + i)
                return carry

            lax.fori_loop(0, each, pair, 0)

        @pl.when(k == first_att + pairs // each)
        def _():
            writes[6].start()
            writes[9].start()
            branch()
            writes[7].start()
            writes[8].start()

        @pl.when(done >= 4 + per)
        def _():
            feed(done - 4 - per)

        return carry

    lax.fori_loop(0, chunks + 2, tick, 0)
    count = cnt[hops]
    weight = rows * (1 << hops) / count
    scale_ref[...] = weight
    writes[0].wait()
    some = 128

    def loss(i, carry):
        at = pl.ds(pl.multiple_of(i * some, some), some)
        bias = par_ref[0:1, pl.ds(pl.multiple_of(8 * width + hidden + i * some, some), some)]
        out_y = x_ref[:, at].astype(F32) + (fy[:, at] + bias)
        g = weight[0:1, :] * valid_ref[...] * (out_y - t_ref[:, at].astype(F32))
        low = g.astype(BF16)
        fy[:, at] = g
        n1[:, at] = low
        n1t[i] = low.T
        sum_ref[0:1, at] = jnp.sum(low.astype(F32), axis=0, keepdims=True)
        return carry

    lax.fori_loop(0, width // some, loss, 0)
    for k in (10, 11, 12):
        writes[k].start()
    for k in range(2, 13):
        if k != 1:
            writes[k].wait()

    def drain(c, carry):
        w_copy(c).wait()
        return carry

    lax.fori_loop(0, chunks, drain, 0)


def forward_pass(master, vec, tokens, targets, valid, seg, replicas, total):
    rows, width = tokens.shape
    half = rows // 2
    stack = master.shape[1]
    chunks = stack // CHUNK
    hidden = (stack - 4 * width) // 2
    replica_bits = replicas.bit_length() - 1
    assert replicas == 1 << replica_bits
    blocks = width // BS
    hops = 3 + replica_bits
    anyspace = pl.BlockSpec(memory_space=pl.ANY)
    vmem = pl.BlockSpec(memory_space=pltpu.VMEM)
    dma = pltpu.SemaphoreType.DMA
    turned = sds((blocks, BS, rows), BF16)
    flat = sds((rows, width), BF16)
    two = sds((2, rows, width), BF16)
    tall = sds((rows, hidden), BF16)
    return pl.pallas_call(
        partial(fwd_kernel, total, replica_bits),
        out_shape=[
            sds((blocks, BS, stack), BF16), turned, turned, turned, turned, flat, two, two, flat, tall, tall,
            sds((rows, width), F32), flat, sds((3, rows, LANES), F32),
            sds((blocks, 2, rows), F32), sds((1, width), F32), sds((1, total), F32), sds((8, LANES), F32),
        ],
        in_specs=[anyspace] + [vmem] * 5,
        out_specs=[anyspace] * 14 + [vmem] * 4,
        scratch_shapes=[
            pltpu.VMEM((blocks, BS, stack), BF16),
            pltpu.VMEM((3, BS, CHUNK), F32),
            pltpu.VMEM((8, 16, LANES), F32),
            pltpu.VMEM((rows, width), BF16),
            pltpu.VMEM((rows, width), BF16),
            pltpu.VMEM((blocks, BS, rows), BF16),
            pltpu.VMEM((blocks, BS, rows), BF16),
            pltpu.VMEM((3, rows, width), BF16),
            pltpu.VMEM((2, rows, width), BF16),
            pltpu.VMEM((rows, hidden), BF16),
            pltpu.VMEM((rows, hidden), BF16),
            pltpu.VMEM((rows, width), BF16),
            pltpu.VMEM((rows, width), F32),
            pltpu.VMEM((5, rows, half), F32),
            pltpu.VMEM((2, rows, LANES), F32),
            pltpu.VMEM((2, rows, 2 * LANES), F32),
            pltpu.VMEM((5, half, half), F32),
            pltpu.VMEM((2 * rows, LANES), BF16),
            pltpu.VMEM((2 * rows, 2 * LANES), BF16),
            pltpu.VMEM((3, rows, LANES), F32),
            pltpu.VMEM((hops + 1, 8, LANES), F32),
            pltpu.VMEM((hops, 8, LANES), F32),
            dma((3,)), dma((chunks,)), dma((8, chunks)), dma((8, chunks)), dma((7,)), dma((7,)),
            dma((2,)), dma((2,)), dma((hops,)), dma((hops,)), dma((13,)),
        ],
        compiler_params=pltpu.CompilerParams(
            collective_id=1, has_side_effects=True, vmem_limit_bytes=59 * MIB
        ),
    )(master, vec, tokens, targets, valid, seg)


def att_bwd_kernel(
    par_ref, q_ref, k_ref, v_ref, ko_ref, vo_ref, g_ref, o_ref, lse_ref, qseg_ref, kseg_ref, c_ref, lo_ref, hi_ref,
    dq_ref, dk_ref, dv_ref, dko_ref, dvo_ref, mask, kpos, vpos, dkpos, dvpos, dqs, qcat, gcat, rowsum,
):
    rows = q_ref.shape[0]
    half = rows // 2
    parity = par_ref[0]

    @pl.when(pl.program_id(0) == 0)
    def _():
        def one(t, carry):
            b, j = key_tile(t, parity)
            quarter = jnp.where(b == 0, parity, 3 - parity)
            kp = j * half + lax.broadcasted_iota(jnp.int32, (half, half), 0)
            qp = quarter * half + lax.broadcasted_iota(jnp.int32, (half, half), 1)
            same = kseg_ref[pl.ds(pl.multiple_of(j * half, half), half), :] == qseg_ref[pl.ds(b, 1), :]
            mask[t] = jnp.where((kp <= qp) & same, BIG, NEG)
            return carry

        lax.fori_loop(0, 5, one, 0)

    place_keys(k_ref, ko_ref, kpos, parity)
    place_keys(v_ref, vo_ref, vpos, parity)
    dkpos[...] = jnp.zeros_like(dkpos)
    dvpos[...] = jnp.zeros_like(dvpos)
    dqs[...] = jnp.zeros_like(dqs)
    scale = HD**-0.5
    for b in range(2):
        at = slice(b * half, (b + 1) * half)
        qcat[b] = split_heads(q_ref[at, :] * jnp.asarray(scale, BF16))
        gs = g_ref[at, :]
        gcat[b] = split_heads(gs)
        prod = (gs.astype(F32) * o_ref[at, :].astype(F32)).T
        rowsum[b, 0:1, :half] = lse_ref[0, 0:1, at]
        rowsum[b, 0:1, half:] = lse_ref[0, 1:2, at]
        rowsum[b, 1:2, :half] = jnp.sum(prod[:HD, :], axis=0, keepdims=True)
        rowsum[b, 1:2, half:] = jnp.sum(prod[HD:, :], axis=0, keepdims=True)

    def tile(t, carry):
        b, j = key_tile(t, parity)
        ks = pl.ds(pl.multiple_of(j * half, half), half)
        keys = kpos[ks, :]
        qh, gh = qcat[b], gcat[b]
        m = mask[t]
        s = dot_nt(keys, qh)
        s = jnp.concatenate([jnp.minimum(s[:, :half], m), jnp.minimum(s[:, half:], m)], axis=1)
        p = jnp.exp(s - rowsum[b, 0:1, :])
        dp = dot_nt(vpos[ks, :], gh)
        ds = (p * (dp - rowsum[b, 1:2, :])).astype(BF16)
        dvpos[ks, :] += dot(p.astype(BF16), gh)
        dkpos[ks, :] += dot(ds, qh)
        dqs[b] += dot(ds, keys, ((0,), (0,)))
        return carry

    lax.fori_loop(0, 5, tile, 0)
    for b in range(2):
        at = slice(b * half, (b + 1) * half)
        dq = join_heads(dqs[b]) * scale
        dq_ref[at, :] = turn(dq, c_ref[at, :], -lo_ref[at, :], -hi_ref[at, :]).astype(BF16)
    for src, mine, theirs in ((dkpos, dk_ref, dko_ref), (dvpos, dv_ref, dvo_ref)):
        for b in range(2):
            at = slice(b * half, (b + 1) * half)
            own = parity if b == 0 else 3 - parity
            other = 1 - parity if b == 0 else 2 + parity
            mine[at, :] = src[pl.ds(pl.multiple_of(own * half, half), half), :].astype(mine.dtype)
            theirs[at, :] = src[pl.ds(pl.multiple_of(other * half, half), half), :].astype(BF16)


def att_bwd(parity, q, kv, kvo, gob, ob, lse, qseg, kseg, tables):
    rows, width = q.shape
    pairs = width // LANES
    half = rows // 2
    col = lambda off: pl.BlockSpec((rows, LANES), lambda p, r: (0, p + off))
    kvc = lambda which: pl.BlockSpec((None, rows, LANES), lambda p, r: (which, 0, p))
    out = sds((rows, width), F32)
    low = sds((rows, width), BF16)
    return call(
        att_bwd_kernel,
        (pairs,),
        [
            col(0), kvc(0), kvc(1), kvc(0), kvc(1), col(0), col(0),
            pl.BlockSpec((1, 2, rows), lambda p, r: (p, 0, 0)),
            whole((2, half)), whole((2 * rows, 1)),
            *[pl.BlockSpec((None, rows, LANES), lambda p, r, k=k: (k, 0, 0)) for k in range(3)],
        ],
        [col(0)] * 5,
        [low, out, out, low, low],
        [
            pltpu.VMEM((5, half, half), F32),
            pltpu.VMEM((2 * rows, LANES), BF16),
            pltpu.VMEM((2 * rows, LANES), BF16),
            pltpu.VMEM((2 * rows, LANES), F32),
            pltpu.VMEM((2 * rows, LANES), F32),
            pltpu.VMEM((2, rows, LANES), F32),
            pltpu.VMEM((2, rows, LANES), BF16),
            pltpu.VMEM((2, rows, LANES), BF16),
            pltpu.VMEM((2, 8, rows), F32),
        ],
        prefetch=1,
        cost=cost(10 * rows * 2 * rows * width, 2 * 16 * rows * width, 2 * rows * rows * width // HD),
    )(parity, q, kv, kv, kvo, kvo, gob, ob, lse, qseg, kseg, tables, tables, tables)


def dgrad_kernel(gb_ref, wo_ref, wd_ref, wu_ref, dg_ref, gob_ref, gub_ref, sum_ref, gn2_ref):
    @pl.when(pl.program_id(0) == 0)
    def _():
        gob_ref[...] = dot_nt(gb_ref[...], wo_ref[...]).astype(BF16)
        gn2_ref[...] = jnp.zeros_like(gn2_ref)

    act = dot(gb_ref[...], wd_ref[...])
    gub = (act * dg_ref[...].astype(F32)).astype(BF16)
    gub_ref[...] = gub
    sum_ref[...] = jnp.sum(gub.astype(F32), axis=0, keepdims=True)
    gn2_ref[...] += dot_nt(gub, wu_ref[...])


def dgrad(gb, w, dg):
    rows, width = gb.shape
    hidden = dg.shape[1]
    cols = 512
    blk = pl.BlockSpec((rows, cols), lambda j: (0, j))
    wblk = lambda off: pl.BlockSpec((width, cols), lambda j: (0, j + off // cols))
    return call(
        dgrad_kernel,
        (hidden // cols,),
        [
            whole((rows, width)), pl.BlockSpec((width, width), lambda j: (0, 3)),
            wblk(4 * width + hidden), wblk(4 * width), blk,
        ],
        [whole((rows, width)), blk, pl.BlockSpec((1, cols), lambda j: (0, j)), whole((rows, width))],
        [sds((rows, width), BF16), sds((rows, hidden), BF16), sds((1, hidden), F32), sds((rows, width), F32)],
        cost=cost(2 * rows * width * (width + 2 * hidden), 2 * (width * (width + 2 * hidden) + 6 * rows * width)),
    )(gb, w, w, w, dg)


def last_kernel(
    dq_ref, dk_ref, dv_ref, dko_ref, dvo_ref, c_ref, lo_ref, hi_ref, w_ref, x_ref, vec_ref, gn2_ref, gy_ref,
    gqkv_ref, in_ref, vg_ref, sum_ref, gn1,
):
    j = pl.program_id(0)
    rows, width = x_ref.shape
    cols = w_ref.shape[1]
    nq = width // cols

    @pl.when(j == 0)
    def _():
        gn1[...] = jnp.zeros_like(gn1)

    @pl.when(j < nq)
    def _():
        gqkv_ref[...] = dq_ref[...]

    @pl.when((j >= nq) & (j < 2 * nq))
    def _():
        for g in range(cols // LANES):
            at = slice(g * LANES, (g + 1) * LANES)
            grad = dk_ref[:, at] + dko_ref[:, at].astype(F32)
            gqkv_ref[:, at] = turn(grad, c_ref[...], -lo_ref[...], -hi_ref[...]).astype(BF16)

    @pl.when(j >= 2 * nq)
    def _():
        gqkv_ref[...] = (dv_ref[...] + dvo_ref[...].astype(F32)).astype(BF16)

    low = gqkv_ref[...]
    sum_ref[...] = jnp.sum(low.astype(F32), axis=0, keepdims=True)
    gn1[...] += dot_nt(low, w_ref[...])

    @pl.when(j == 3 * nq - 1)
    def _():
        step = 64
        vg_ref[...] = jnp.zeros_like(vg_ref)

        def chunk(i, carry):
            at = pl.ds(pl.multiple_of(i * step, step), step)
            xh, rstd = normed(x_ref[at, :].astype(F32))
            total = gy_ref[at, :]
            sums = []
            for g_n, gain in ((gn1[at, :], vec_ref[0:1, :]), (gn2_ref[at, :], vec_ref[2:3, :])):
                sums.append(jnp.sum(g_n * xh, axis=0, keepdims=True))
                sums.append(jnp.sum(g_n, axis=0, keepdims=True))
                e = g_n * gain
                mean = jnp.mean(e, axis=-1, keepdims=True)
                along = jnp.mean(e * xh, axis=-1, keepdims=True)
                total = total + rstd * (e - mean - xh * along)
            in_ref[at, :] = total
            vg_ref[...] += jnp.concatenate(sums, axis=0)
            return carry

        lax.fori_loop(0, rows // step, chunk, 0)


def last(dq, dk, dv, dko, dvo, tables, w, x, vec4, gn2, gy):
    rows, width = x.shape
    cols = 512
    nq = width // cols
    at = lambda lo: pl.BlockSpec((rows, cols), lambda j: (0, jnp.clip(j - lo * nq, 0, nq - 1)))
    return call(
        last_kernel,
        (3 * nq,),
        [
            at(0), at(1), at(2), at(1), at(2),
            *[pl.BlockSpec((None, rows, LANES), lambda j, k=k: (k, 0, 0)) for k in range(3)],
            pl.BlockSpec((width, cols), lambda j: (0, j)),
            whole((rows, width)), whole(vec4.shape), whole((rows, width)), whole((rows, width)),
        ],
        [
            pl.BlockSpec((rows, cols), lambda j: (0, j)), whole((rows, width)), whole((4, width)),
            pl.BlockSpec((1, cols), lambda j: (0, j)),
        ],
        [sds((rows, 3 * width), BF16), sds((rows, width), F32), sds((4, width), F32), sds((1, 3 * width), F32)],
        [pltpu.VMEM((rows, width), F32)],
        cost=cost(6 * rows * width * width, 2 * (3 * width * width + 20 * rows * width)),
    )(dq, dk, dv, dko, dvo, tables, tables, tables, w, x, vec4, gn2, gy)


def update_kernel(f_ref, g_ref, ls_ref, rs_ref, lr_ref, rr_ref, m_ref, nl_ref, nr_ref, nm_ref, mc_ref):
    factor = f_ref[0, 0]
    half_sq = 0.5 * factor * factor
    for k in range(ls_ref.shape[1]):
        at = slice(k * BS, (k + 1) * BS)
        g = g_ref[:, at]
        gt = g.T
        nl_ref[0, k] = 0.5 * ls_ref[0, k] + half_sq * dot(g, gt)
        nr_ref[0, k] = 0.5 * rs_ref[0, k] + half_sq * dot(gt, g)
        tb = (g.astype(F32) * factor).astype(BF16)
        mb = dot(lr_ref[0, k], tb).astype(BF16)
        new = m_ref[:, at] - LEARN * dot(mb, rr_ref[0, k])
        nm_ref[:, at] = new
        mc_ref[:, at] = new.astype(BF16)


def update(factor, g, ls, rs, lr, rr, m):
    rows, total = g.shape
    count = ls.shape[1]
    per = 8
    blk = pl.BlockSpec((1, per, BS, BS), lambda j: (0, j, 0, 0))
    col = pl.BlockSpec((rows, per * BS), lambda j: (0, j))
    return call(
        update_kernel,
        (count // per,),
        [pl.BlockSpec(memory_space=pltpu.SMEM), col, blk, blk, blk, blk, col],
        [blk, blk, col, col],
        [sds(ls.shape, F32), sds(rs.shape, F32), sds(m.shape, F32), sds(m.shape, BF16)],
        cost=cost(8 * rows * total * BS, rows * total * 32),
    )(factor, g, ls, rs, lr, rr, m)


PAIR = 1024
TILE = PAIR // 2


def reduce_kernel(plan, levels, replica_bits, *refs):
    groups = len(plan)
    pairs = sum(plan)
    at_refs, b_refs = refs[:groups], refs[groups : 2 * groups]
    v_ref, g_out, vec_out, sq_out = refs[2 * groups : 2 * groups + 4]
    (a_own, a_oth, b_own, b_oth, s1, r1, r2, zs, gs, vr, vd, sq, sq_in,
     sem_l, sem_b, sem_as, sem_ar, sem_bs, sem_br, sem_1s, sem_1r, sem_2s, sem_2r,
     sem_zs, sem_zr, sem_gs, sem_gr, sem_vs, sem_vr, sem_qs, sem_qr, sem_o) = refs[2 * groups + 4 :]
    s = lax.axis_index("shard")
    z = lax.axis_index("dp")
    core, x, y = bits_of(s, 3)
    zb = bits_of(z, replica_bits)
    to_core = {"shard": s + 1 - 2 * core}
    to_x = {"shard": s + 2 - 4 * x}
    to_y = {"shard": s + 4 - 8 * y}
    to_z = [{"dp": z + (1 - 2 * zb[l]) * (1 << l)} for l in range(replica_bits)]
    peers = [to_core, to_x, to_y] + to_z

    meet(peers)

    first = [sum(plan[:w]) for w in range(groups + 1)]

    def a_local(w):
        return pltpu.make_async_copy(at_refs[w].at[:, core], a_own.at[w], sem_l.at[w])

    def a_send(w):
        return remote(at_refs[w].at[:, 1 - core], a_oth.at[w], sem_as.at[w], sem_ar.at[w], to_core)

    def b_cols(w, i):
        return b_refs[w].at[:, pl.ds(pl.multiple_of((i - first[w]) * PAIR, PAIR), PAIR)]

    def b_send(w, i):
        return remote(b_cols(w, i), b_oth.at[i], sem_bs.at[i], sem_br.at[i], to_core)

    def b_local(w, i):
        return pltpu.make_async_copy(b_cols(w, i), b_own.at[i % 2], sem_b.at[i % 2])

    for w in range(groups):
        a_local(w).start()
        a_send(w).start()
        if w == 0:
            b_local(0, 0).start()

        def launch(i, carry, w=w):
            b_send(w, i).start()
            return carry

        lax.fori_loop(first[w], first[w + 1], launch, 0)

    v4 = v_ref
    vecs = [
        (v4.at[:, :, 1 - core], vr.at[0, :, :], to_core),
        (vr.at[0, :, 1 - x], vr.at[1, 0, :], to_x),
        (vr.at[1, 0, 1 - y], vr.at[1, 1, 0], to_y),
    ]

    def v_copy(k):
        if k < 3:
            src, dst, peer = vecs[k]
        else:
            src, dst, peer = vd.at[2 * (k - 3)], vd.at[2 * (k - 3) + 1], to_z[k - 3]
        return remote(src, dst, sem_vs.at[k], sem_vr.at[k], peer)

    def v_done(k):
        v_copy(k).wait()
        if k == 0:
            vr[0] = vr[0] + v4[:, :, core]
        elif k == 1:
            vr[1, 0] = vr[1, 0] + vr[0, :, x]
        else:
            if k == 2:
                total = vr[1, 1, 0] + vr[1, 0, y]
            else:
                total = vd[2 * (k - 3)] + vd[2 * (k - 3) + 1]
            vd[2 * (k - 2)] = total

    v_hops = 3 + replica_bits
    v_copy(0).start()
    sq[...] = jnp.zeros_like(sq)

    def copy1(i, t):
        src = s1.at[i, t, :, 1 - x] if t == 0 else s1.at[i, t, 1 - y]
        return remote(src, r1.at[i, t], sem_1s.at[i, t], sem_1r.at[i, t], to_x if t == 0 else to_y)

    def copy2(i, t):
        bit = y if t == 0 else x
        return remote(
            r1.at[i, t, 1 - bit], r2.at[i, :, t * TILE : (t + 1) * TILE],
            sem_2s.at[i, t], sem_2r.at[i, t], to_y if t == 0 else to_x,
        )

    starts = [0]
    for l in range(levels):
        starts.append(starts[l] + (BS >> (l + 1)))

    def z_rows(l):
        return pl.ds(starts[l], BS >> (l + 1))

    def level_src(i, l, half):
        size = BS >> (l + 1)
        off = pl.multiple_of(half * size, size)
        if l == 0:
            return r2.at[i, pl.ds(off, size)]
        return zs.at[i, pl.ds(pl.multiple_of(starts[l - 1] + off, size), size)]

    def copy_z(i, l):
        return remote(
            level_src(i, l, 1 - zb[l]), zs.at[i, z_rows(l)], sem_zs.at[i, l], sem_zr.at[i, l], to_z[l]
        )

    def g_rows(l, mine):
        base = sum((zb[m] * (BS >> (m + 1)) for m in range(l)), 0)
        size = BS >> (l + 1)
        half = zb[l] if mine else 1 - zb[l]
        return pl.ds(pl.multiple_of(base + half * size, size), size)

    def copy_g(i, l):
        return remote(gs.at[i, g_rows(l, True)], gs.at[i, g_rows(l, True)], sem_gs.at[i, l], sem_gr.at[i, l], to_z[l])

    def out_cols(i):
        total = g_out.shape[1] // PAIR
        spot = total - first[1] + i
        spot = jnp.where(i >= first[1], i - first[1] + plan[3], spot)
        spot = jnp.where(i >= first[3], i - first[3], spot)
        return pl.ds(pl.multiple_of(spot * PAIR, PAIR), PAIR)

    def out_copy(i):
        src = gs.at[i] if levels else r2.at[i]
        return pltpu.make_async_copy(src, g_out.at[:, out_cols(i)], sem_o.at[i])

    def stage_a(i):
        group = sum((jnp.where(i >= first[w], 1, 0) for w in range(1, groups)), 0)
        for w in range(groups):
            @pl.when(i == first[w])
            def _():
                a_local(w).wait()
                a_send(w).wait()

            @pl.when((i + 1 >= first[w]) & (i + 1 < first[w + 1]))
            def _():
                b_local(w, i + 1).start()

        slot = i % 2
        pltpu.make_async_copy(b_oth.at[i], b_own.at[slot], sem_b.at[slot]).wait()
        remote(b_own.at[slot], b_oth.at[i], sem_bs.at[i], sem_br.at[i], to_core).wait()
        size = 4 * BS
        own = a_own[group].reshape(size, a_own.shape[-1])
        oth = a_oth[group].reshape(size, a_oth.shape[-1])
        for t in range(2):
            at = slice(t * TILE, (t + 1) * TILE)
            acc = dot(own, b_own[slot, :, at]) + dot(oth, b_oth[i, :, at])
            s1[i, t] = acc.astype(BF16).reshape(2, 2, BS, TILE)
            copy1(i, t).start()

    def stage_b(i):
        for t in range(2):
            copy1(i, t).wait()
            kept = s1[i, t, :, x] if t == 0 else s1[i, t, y]
            r1[i, t] = (r1[i, t].astype(F32) + kept.astype(F32)).astype(BF16)
            copy2(i, t).start()

    def stage_c(i):
        for t in range(2):
            copy2(i, t).wait()
            at = slice(t * TILE, (t + 1) * TILE)
            bit = y if t == 0 else x
            r2[i, :, at] = (r2[i, :, at].astype(F32) + r1[i, t, bit].astype(F32)).astype(BF16)
        if levels:
            copy_z(i, 0).start()
        else:
            out_copy(i).start()

    def stage_z(l):
        def run(i):
            copy_z(i, l).wait()
            total = zs[i, z_rows(l)].astype(F32) + level_src(i, l, zb[l])[...].astype(F32)
            if l + 1 < levels:
                zs[i, z_rows(l)] = total.astype(BF16)
                copy_z(i, l + 1).start()
            else:
                gs[i, g_rows(l, True)] = total.astype(BF16)
                copy_g(i, l).start()
        return run

    def stage_g(l):
        def run(i):
            copy_g(i, l).wait()
            if l:
                copy_g(i, l - 1).start()
            else:
                part = gs[i].astype(F32)
                part = jnp.sum((part * part).reshape(BS // 8, 8, PAIR), axis=0)
                sq[0] += sum(part[:, g * LANES : (g + 1) * LANES] for g in range(PAIR // LANES))
                out_copy(i).start()
        return run

    stages = [stage_a, stage_b, stage_c]
    stages += [stage_z(l) for l in range(levels)] + [stage_g(l) for l in reversed(range(levels))]
    lags = len(stages)

    def step(i, carry):
        for lag, stage in enumerate(stages):
            @pl.when((i >= lag) & (i < pairs + lag))
            def _():
                stage(i - lag)

        for k in range(v_hops):
            @pl.when(i == k + 1)
            def _():
                v_done(k)
                if k + 1 < v_hops:
                    v_copy(k + 1).start()
        return carry

    lax.fori_loop(0, pairs + lags - 1, step, 0)
    total = vd[2 * replica_bits]
    vec_out[...] = total
    rows13 = lax.broadcasted_iota(jnp.int32, total.shape, 0) < 13
    square = jnp.where(rows13, total * total, 0.0)
    sq[0] += square[0:8] + square[8:16]
    for k, peer in enumerate((to_core, to_x, to_y)):
        hop = remote(sq.at[k], sq_in.at[k], sem_qs.at[k], sem_qr.at[k], peer)
        hop.start()
        hop.wait()
        sq[k + 1] = sq[k] + sq_in[k]
    sq_out[...] = sq[3]

    def drain(i, carry):
        out_copy(i).wait()
        return carry

    lax.fori_loop(0, pairs, drain, 0)


def reduce_grads(ats, bs, vec, replicas):
    plan = [b.shape[1] // PAIR for b in bs]
    pairs = sum(plan)
    tokens = bs[0].shape[0]
    replica_bits = replicas.bit_length() - 1
    assert replicas == 1 << replica_bits
    levels = replica_bits if replicas <= 8 else 0
    groups = len(plan)
    dma = pltpu.SemaphoreType.DMA
    lv, vh = max(levels, 1), 3 + replica_bits
    scratch = [
        pltpu.VMEM((groups, 4, BS, tokens), BF16),
        pltpu.VMEM((groups, 4, BS, tokens), BF16),
        pltpu.VMEM((2, tokens, PAIR), BF16),
        pltpu.VMEM((pairs, tokens, PAIR), BF16),
        pltpu.VMEM((pairs, 2, 2, 2, BS, TILE), BF16),
        pltpu.VMEM((pairs, 2, 2, BS, TILE), BF16),
        pltpu.VMEM((pairs, BS, PAIR), BF16),
        pltpu.VMEM((pairs, BS if levels else 16, PAIR), BF16),
        pltpu.VMEM((pairs if levels else 1, BS, PAIR), BF16),
        pltpu.VMEM((2, 2, 2, 16, LANES), F32),
        pltpu.VMEM((2 * replica_bits + 2, 16, LANES), F32),
        pltpu.VMEM((4, 8, LANES), F32),
        pltpu.VMEM((3, 8, LANES), F32),
        dma((groups,)), dma((2,)), dma((groups,)), dma((groups,)), dma((pairs,)), dma((pairs,)),
        dma((pairs, 2)), dma((pairs, 2)), dma((pairs, 2)), dma((pairs, 2)),
        dma((pairs, lv)), dma((pairs, lv)), dma((pairs, lv)), dma((pairs, lv)),
        dma((vh,)), dma((vh,)), dma((3,)), dma((3,)), dma((pairs,)),
    ]
    anyspace = pl.BlockSpec(memory_space=pl.ANY)
    vmem = pl.BlockSpec(memory_space=pltpu.VMEM)
    return pl.pallas_call(
        partial(reduce_kernel, plan, levels, replica_bits),
        out_shape=[
            sds((BS, pairs * PAIR), BF16), sds((16, LANES), F32), sds((8, LANES), F32)
        ],
        in_specs=[anyspace] * (2 * groups) + [vmem],
        out_specs=[anyspace, vmem, vmem],
        scratch_shapes=scratch,
        compiler_params=pltpu.CompilerParams(
            collective_id=0, has_side_effects=True, vmem_limit_bytes=58 * MIB
        ),
    )(*[a.reshape(4, 2, BS, tokens) for a in ats], *bs, vec)


def body(
    tokens, targets, segments, valid, master, vectors, left_stat, right_stat, left_root, right_root, vector_stat,
):
    rows, width = tokens.shape
    stack = master.shape[1]
    hidden = (stack - 4 * width) // 2
    half = rows // 2
    shards = lax.axis_size("shard")
    replicas = lax.axis_size("dp")
    index = lax.axis_index("shard")
    parity = index % 2
    par = parity.astype(jnp.int32).reshape(1)
    swap = [(i, i ^ 1) for i in range(shards)]

    start = (index - parity) * rows
    sequence = lax.dynamic_slice_in_dim(segments, start, 2 * rows).reshape(4, half)
    key_seg = jnp.stack([sequence[0], sequence[2], sequence[3], sequence[1]])
    own_seg = lax.dynamic_slice_in_dim(segments, index * rows, rows)

    own_len = vectors.shape[0]
    lines = own_len // LANES
    vec = jnp.pad(vectors.reshape(lines, LANES), ((0, 16 - lines), (0, 0)))
    (weights, n1t, n2t, obt, gbt, q, kv, kvo, ob, hb, dg, gy, gb, tables, lse, gb_sum, params, scales) = forward_pass(
        master, vec, tokens, targets, valid.astype(F32).reshape(rows, 1), segments.reshape(-1, 1, half), replicas,
        own_len * shards,
    )
    weights = weights.reshape(width, stack)
    vec4 = params[0, : 4 * width].reshape(4, width)
    gob, gub, gub_sum, gn2 = dgrad(gb, weights, dg)

    dq, dk, dv, dk_o, dv_o = att_bwd(
        par, q, kv, kvo, gob, ob, lse, own_seg.reshape(2, half), key_seg.reshape(2 * rows, 1), tables
    )
    dk_r = lax.ppermute(dk_o, "shard", swap)
    dv_r = lax.ppermute(dv_o, "shard", swap)
    gqkv, input_grad, vec_grad, gqkv_sum = last(
        dq, dk, dv, dk_r, dv_r, tables, weights, tokens, vec4, gn2, gy
    )
    vector_grad = jnp.concatenate(
        [vec_grad.reshape(-1), gqkv_sum.reshape(-1), gb_sum.reshape(-1), gub_sum.reshape(-1), gb_sum.reshape(-1)]
    ).reshape(shards, lines, LANES)
    packed = jnp.pad(vector_grad, ((0, 0), (0, 16 - lines), (0, 0))).reshape(2, 2, 2, 16, LANES)
    grads, vec_total, squares = reduce_grads((gbt, obt, n2t, n1t), (hb, gb, gub, gqkv), packed, replicas)
    own_vector = vec_total[:lines].reshape(own_len)
    if replicas <= 8:
        square_sum = jnp.sum(squares)
    else:
        grads = lax.psum_scatter(grads, "dp", scatter_dimension=1, tiled=True)
        grads = lax.all_gather(grads, "dp", axis=1, tiled=True)
        square_sum = jnp.sum(squares) + lax.psum(jnp.sum(jnp.square(grads.astype(F32))), "shard")
    grad_norm = jnp.sqrt(square_sum)
    factor = jnp.minimum(1.0, math.sqrt(width * stack / BS) / grad_norm)
    new_left, new_right, new_master, master_copy = update(
        factor.reshape(1, 1), grads, left_stat, right_stat, left_root, right_root, master
    )
    scaled_vec = own_vector * factor
    new_vstat = 0.5 * vector_stat + 0.5 * scaled_vec * scaled_vec
    new_vectors = vectors - LEARN_VEC * scaled_vec / jnp.sqrt(new_vstat)
    return (input_grad, grad_norm, new_left, new_right, new_master, master_copy, new_vectors, new_vstat)


def solution(mesh):
    rows = P(("dp", "shard"), None)
    quad = P("shard", None, None, None)
    return jax.shard_map(
        body,
        mesh=mesh,
        in_specs=(
            rows, rows, P("dp"), P(("dp", "shard")), P("shard", None), P("shard"), quad, quad, quad, quad, P("shard"),
        ),
        out_specs=(rows, P(), quad, quad, P("shard", None), P("shard", None), P("shard"), P("shard")),
        check_vma=False,
    )
```

```python
from functools import partial
import math

import jax
import jax.numpy as jnp
from jax import lax
from jax.experimental import pallas as pl
from jax.experimental.pallas import tpu as pltpu
from jax.sharding import PartitionSpec as P

HD = 64
ROT = 16
BS = 128
LANES = 128
EPS = 1e-05
NEG = -1e30
BIG = 3e38
LEARN = 0.5
LEARN_VEC = 0.15
F32 = jnp.float32
BF16 = jnp.bfloat16
MIB = 1 << 20


def dot(a, b, dims=((1,), (0,))):
    return lax.dot_general(a, b, (dims, ((), ())), preferred_element_type=F32)


def dot_nt(a, b):
    return dot(a, b, ((1,), (1,)))


def call(kernel, grid, in_specs, out_specs, out_shape, scratch=(), vmem=48, prefetch=0, cost=None):
    return pl.pallas_call(
        kernel,
        out_shape=out_shape,
        grid_spec=pltpu.PrefetchScalarGridSpec(
            num_scalar_prefetch=prefetch,
            grid=grid,
            in_specs=in_specs,
            out_specs=out_specs,
            scratch_shapes=list(scratch),
        ),
        compiler_params=pltpu.CompilerParams(
            vmem_limit_bytes=vmem * MIB, dimension_semantics=("arbitrary",) * len(grid)
        ),
        cost_estimate=cost,
    )


def cost(flops, nbytes, trans=0):
    return pl.CostEstimate(flops=int(flops), bytes_accessed=int(nbytes), transcendentals=int(trans))


def whole(shape):
    rank = len(shape)
    return pl.BlockSpec(shape, lambda *g: (0,) * rank)


def sds(shape, dtype):
    return jax.ShapeDtypeStruct(shape, dtype)


def normed(x):
    mean = jnp.mean(x, axis=-1, keepdims=True)
    centred = x - mean
    rstd = lax.rsqrt(jnp.mean(centred * centred, axis=-1, keepdims=True) + EPS)
    return centred * rstd, rstd


def turn(values, c, lo, hi):
    return values * c + pltpu.roll(values, LANES - ROT // 2, 1) * lo + pltpu.roll(values, ROT // 2, 1) * hi


def place_keys(own_ref, other_ref, out_ref, parity):
    half = own_ref.shape[0] // 2
    for ref, who in ((own_ref, parity), (other_ref, 1 - parity)):
        for b in range(2):
            quarter = who if b == 0 else 3 - who
            out_ref[pl.ds(pl.multiple_of(quarter * half, half), half), :] = ref[b * half : (b + 1) * half, :]


def key_tile(t, parity):
    first = parity + 1
    b = jnp.where(t >= first, 1, 0)
    return b, t - b * first


def split_heads(pair):
    lane = lax.broadcasted_iota(jnp.int32, pair.shape, 1)
    zero = jnp.zeros_like(pair)
    return jnp.concatenate([jnp.where(lane < HD, pair, zero), jnp.where(lane >= HD, pair, zero)], axis=0)


def join_heads(both):
    half = both.shape[0] // 2
    lane = lax.broadcasted_iota(jnp.int32, (half, LANES), 1)
    return jnp.where(lane < HD, both[:half], both[half:])


CHUNK = 1024


def bits_of(index, count):
    return [(index // (1 << b)) % 2 for b in range(count)]


def flipped(bits, mask):
    return sum(((1 - bit) if (mask >> k) & 1 else bit) * (1 << k) for k, bit in enumerate(bits))


def remote(src, dst, send, recv, peer):
    return pltpu.make_async_remote_copy(
        src_ref=src, dst_ref=dst, send_sem=send, recv_sem=recv, device_id=peer, device_id_type=pl.DeviceIdType.MESH
    )


def meet(peers):
    barrier = pltpu.get_barrier_semaphore()
    for peer in peers:
        pl.semaphore_signal(barrier, inc=1, device_id=peer, device_id_type=pl.DeviceIdType.MESH)
    pl.semaphore_wait(barrier, len(peers))


def column(row):
    return jnp.broadcast_to(row.astype(F32), (LANES, row.shape[1])).T


def rotary_tables(parity, rows, c_ref, lo_ref, hi_ref):
    half = rows // 2
    lane = lax.broadcasted_iota(jnp.int32, (1, LANES), 1) % HD
    frequency = jnp.zeros((1, LANES), F32)
    for k in range(ROT // 2):
        value = 10000.0 ** (-2.0 * k / ROT)
        frequency = jnp.where((lane < ROT) & (lane % (ROT // 2) == k), value, frequency)
    step = 64

    def chunk(i, carry):
        row = i * step + lax.broadcasted_iota(jnp.int32, (step, LANES), 0)
        late = (i * step) // half
        quarter = parity + late * (3 - 2 * parity)
        position = (row - late * half + quarter * half).astype(F32)
        grid = position * frequency
        at = pl.ds(pl.multiple_of(i * step, step), step)
        sine = jnp.sin(grid)
        c_ref[at, :] = jnp.cos(grid)
        lo_ref[at, :] = jnp.where(lane < ROT // 2, -sine, 0.0)
        hi_ref[at, :] = jnp.where((lane >= ROT // 2) & (lane < ROT), sine, 0.0)
        return carry

    lax.fori_loop(0, rows // step, chunk, 0)


def fwd_kernel(
    total, replica_bits,
    m_ref, v_ref, x_ref, t_ref, valid_ref, seg_ref,
    w_out, n1t_out, n2t_out, obt_out, gbt_out, q_out, kv_out, kvo_out, ob_out, hb_out, dg_out, gy_out, gb_out, tab_out,
    lse_ref, sum_ref, par_ref, scale_ref,
    w, stage, vbuf, n1, n2, n1t, n2t, qkv, kvo, hb, dg, ob, fy, sc, top, acc, mask, kpos, vpos, tab, cnt, cnt_in,
    sem_m, sem_w, sem_s, sem_r, sem_vs, sem_vr, sem_ks, sem_kr, sem_cs, sem_cr, sem_o,
):
    rows, width = x_ref.shape
    half = rows // 2
    stack = m_ref.shape[1]
    chunks = stack // CHUNK
    hidden = (stack - 4 * width) // 2
    per = hidden // CHUNK
    s = lax.axis_index("shard")
    z = lax.axis_index("dp")
    sb = bits_of(s, 3)
    zb = bits_of(z, replica_bits)
    core, x, y = sb
    parity = core
    to = [{"shard": flipped(sb, k)} for k in range(8)]
    to_z = [{"dp": z + (1 - 2 * zb[l]) * (1 << l)} for l in range(replica_bits)]
    blk = [flipped(sb, k) for k in range(8)]
    CORE, XX, YY = 1, 2, 4

    def load(c):
        return pltpu.make_async_copy(m_ref.at[:, c * CHUNK : (c + 1) * CHUNK], stage.at[c % 3], sem_m.at[c % 3])

    for c in range(3):
        load(c).start()
    meet(to[1:] + to_z)

    vbuf[pl.ds(s, 1)] = v_ref[...].reshape(1, 16, LANES)
    v_sends = [remote(v_ref, vbuf.at[s], sem_vs.at[k - 1], sem_vr.at[k - 1], to[k]) for k in range(1, 8)]
    for copy in v_sends:
        copy.start()

    def cols(c):
        return pl.ds(pl.multiple_of(c * CHUNK, CHUNK), CHUNK)

    def copy(kind, c):
        at = cols(c)
        top_half, low_half = pl.ds(0, BS // 2), pl.ds(BS // 2, BS // 2)
        if kind < 3:
            ref, peer = w.at[s, :, at], to[(XX, YY, CORE)[kind]]
        elif kind == 3:
            ref, peer = w.at[blk[XX], top_half, at], to[YY]
        elif kind == 4:
            ref, peer = w.at[blk[YY], low_half, at], to[XX]
        else:
            ref, peer = w.at[blk[(XX, YY, XX + YY)[kind - 5]], :, at], to[CORE]
        return remote(ref, ref, sem_s.at[kind, c], sem_r.at[kind, c], peer)

    def send(c):
        for kind in range(3):
            copy(kind, c).start()

    def forward(c):
        copy(0, c).wait()
        copy(1, c).wait()
        for kind in (3, 4, 5, 6):
            copy(kind, c).start()

    def corner(c):
        copy(3, c).wait()
        copy(4, c).wait()
        copy(7, c).start()

    def w_copy(c):
        return pltpu.make_async_copy(w.at[:, :, cols(c)], w_out.at[:, :, cols(c)], sem_w.at[c])

    def finish(c):
        for kind in (2, 5, 6, 7):
            copy(kind, c).wait()
        w_copy(c).start()

    for c in range(chunks):
        load(c).wait()
        w[pl.ds(s, 1), :, c * CHUNK : (c + 1) * CHUNK] = stage[c % 3].astype(BF16).reshape(1, BS, CHUNK)
        if c + 3 < chunks:
            load(c + 3).start()
        if c < 2:
            send(c)

    def hop(k):
        return remote(cnt.at[k], cnt_in.at[k], sem_cs.at[k], sem_cr.at[k], ([to[1], to[2], to[4]] + to_z)[k])

    hops = 3 + replica_bits
    cnt[0] = jnp.full((8, LANES), jnp.sum(valid_ref[...]), F32)
    hop(0).start()

    rotary_tables(parity, rows, tab.at[0], tab.at[1], tab.at[2])
    for copy_v in v_sends:
        copy_v.wait()
    lines = total // (8 * LANES)
    for k in range(8):
        block = vbuf[k].astype(BF16).astype(F32)
        for r in range(lines):
            flat = (k * lines + r) * LANES
            par_ref[0:1, flat : flat + LANES] = block[r : r + 1, :]

    def param(start, size):
        return par_ref[0:1, start : start + size]

    step = 128

    def norms(i, carry):
        at = pl.ds(pl.multiple_of(i * step, step), step)
        xh, _ = normed(x_ref[at, :].astype(F32))
        one = (xh * param(0, width) + param(width, width)).astype(BF16)
        two = (xh * param(2 * width, width) + param(3 * width, width)).astype(BF16)
        n1[at, :] = one
        n2[at, :] = two
        for b in range(width // BS):
            n1t[b, :, at] = one[:, b * BS : (b + 1) * BS].T
            n2t[b, :, at] = two[:, b * BS : (b + 1) * BS].T
        return carry

    lax.fori_loop(0, rows // step, norms, 0)

    def out(k, src, dst):
        return pltpu.make_async_copy(src, dst, sem_o.at[k])

    writes = [
        out(0, n1t, n1t_out), out(1, n2t, n2t_out), out(2, tab, tab_out), out(3, qkv.at[0], q_out),
        out(4, qkv.at[pl.ds(1, 2)], kv_out), out(5, kvo, kvo_out), out(6, ob, ob_out), out(7, hb, hb_out),
        out(8, dg, dg_out), out(9, n2t, obt_out), out(10, n1t, gbt_out), out(11, n1, gb_out), out(12, fy, gy_out),
    ]
    for k in range(3):
        writes[k].start()

    first_row = 4 * (s // 2)

    def see(t, carry):
        b, j = key_tile(t, parity)
        quarter = jnp.where(b == 0, parity, 3 - parity)
        qrow = first_row + 2 * parity + b
        krow = first_row + jnp.where(j == 0, 0, jnp.where(j == 3, 1, j + 1))
        qseg = column(seg_ref[qrow])
        for g in range(half // LANES):
            kseg = seg_ref[krow][:, g * LANES : (g + 1) * LANES].astype(F32)
            qpos = quarter * half + lax.broadcasted_iota(jnp.int32, (half, LANES), 0)
            kp = j * half + g * LANES + lax.broadcasted_iota(jnp.int32, (half, LANES), 1)
            mask[t, :, g * LANES : (g + 1) * LANES] = jnp.where((kp <= qpos) & (qseg == kseg), BIG, NEG)
        return carry

    lax.fori_loop(0, 5, see, 0)
    for j in range(4):
        vpos[j * half : (j + 1) * half, LANES:] = jnp.ones((half, LANES), BF16)

    def kv_send(m):
        return remote(qkv.at[m], kvo.at[m - 1], sem_ks.at[m - 1], sem_kr.at[m - 1], to[CORE])

    sub = 512

    def project(m):
        def part(i, carry):
            off = pl.multiple_of(m * CHUNK + i * sub, sub)
            wide = w[:, :, pl.ds(off, sub)].reshape(width, sub)
            proj = dot(n1[...], wide) + par_ref[0:1, pl.ds(pl.multiple_of(4 * width + off, sub), sub)]
            turned = m < 2
            for g in range(sub // LANES):
                piece = proj[:, g * LANES : (g + 1) * LANES]
                piece = jnp.where(turned, turn(piece, tab[0], tab[1], tab[2]), piece)
                qkv[m, :, pl.ds(pl.multiple_of(i * sub + g * LANES, LANES), LANES)] = piece.astype(BF16)
            return carry

        lax.fori_loop(0, CHUNK // sub, part, 0)

    def upward(k):
        def part(i, carry):
            off = pl.multiple_of(k * CHUNK + i * sub, sub)
            wide = w[:, :, pl.ds(pl.multiple_of(4 * width + off, sub), sub)].reshape(width, sub)
            bias = par_ref[0:1, pl.ds(pl.multiple_of(8 * width + off, sub), sub)]
            wide_u = dot(n2[...], wide) + bias
            for g in range(sub // LANES):
                u = wide_u[:, g * LANES : (g + 1) * LANES]
                cdf = 0.5 * (1.0 + lax.erf(u * (1.0 / math.sqrt(2.0))))
                pdf = jnp.exp(-0.5 * u * u) * (1.0 / math.sqrt(2.0 * math.pi))
                at = pl.ds(pl.multiple_of(off + g * LANES, LANES), LANES)
                hb[:, at] = (u * cdf).astype(BF16)
                dg[:, at] = (cdf + u * pdf).astype(BF16)
            return carry

        lax.fori_loop(0, CHUNK // sub, part, 0)

    def branch():
        def part(i, carry):
            at = pl.ds(pl.multiple_of(i * sub, sub), sub)
            wide = w[:, :, pl.ds(pl.multiple_of(3 * width + i * sub, sub), sub)].reshape(width, sub)
            bias = par_ref[0:1, pl.ds(pl.multiple_of(7 * width + i * sub, sub), sub)]
            fy[:, at] = dot(ob[...], wide) + bias
            return carry

        lax.fori_loop(0, width // sub, part, 0)

    def feed(k):
        def part(i, carry):
            at = pl.ds(pl.multiple_of(i * sub, sub), sub)
            off = pl.ds(pl.multiple_of(4 * width + hidden + k * CHUNK, CHUNK), CHUNK)
            tall = w[pl.ds(i * (sub // BS), sub // BS), :, off].reshape(sub, CHUNK)
            fy[:, at] += dot_nt(hb[:, pl.ds(pl.multiple_of(k * CHUNK, CHUNK), CHUNK)], tall)
            return carry

        lax.fori_loop(0, width // sub, part, 0)

    scale = jnp.asarray(HD**-0.5, BF16)

    def attend(p):
        lanes = pl.ds(pl.multiple_of(p * LANES, LANES), LANES)
        place_keys(qkv.at[1, :, lanes], kvo.at[0, :, lanes], kpos, parity)
        place_keys(qkv.at[2, :, lanes], kvo.at[1, :, lanes], vpos.at[:, 0:LANES], parity)
        top[...] = jnp.full_like(top, NEG)
        acc[...] = jnp.zeros_like(acc)

        def score(t, carry):
            b, j = key_tile(t, parity)
            both = split_heads(qkv[0, pl.ds(pl.multiple_of(b * half, half), half), lanes] * scale)
            keys = kpos[pl.ds(pl.multiple_of(j * half, half), half), :]
            got = dot_nt(both, keys)
            m = mask[t]
            got = jnp.concatenate([jnp.minimum(got[:half], m), jnp.minimum(got[half:], m)], axis=0)
            sc[t] = got
            best = top[b]
            for g in range(half // LANES):
                best = jnp.maximum(best, got[:, g * LANES : (g + 1) * LANES])
            top[b] = best
            return carry

        lax.fori_loop(0, 5, score, 0)
        for b in range(2):
            top[b] = jnp.broadcast_to(jnp.max(top[b], axis=1, keepdims=True), top.shape[1:])

        def weigh(t, carry):
            b, j = key_tile(t, parity)
            best = top[b]
            prob = jnp.exp(sc[t] - jnp.concatenate([best] * (half // LANES), axis=1)).astype(BF16)
            acc[b] += dot(prob, vpos[pl.ds(pl.multiple_of(j * half, half), half), :])
            return carry

        lax.fori_loop(0, 5, weigh, 0)
        for b in range(2):
            at = slice(b * half, (b + 1) * half)
            den = acc[b, :, LANES:]
            lse = (top[b] + jnp.log(den)).T[0:1, :]
            lse_ref[p, 0:1, at] = lse[:, :half]
            lse_ref[p, 1:2, at] = lse[:, half:]
            got = join_heads(acc[b, :, :LANES] / den).astype(BF16)
            ob[at, lanes] = got
            n2t[p, :, at] = got.T

    pairs = width // LANES
    first_att = 6
    each = 2

    def tick(k, carry):
        @pl.when(k < chunks)
        def _():
            forward(k)

        @pl.when(k + 2 < chunks)
        def _():
            send(k + 2)

        @pl.when((k >= 1) & (k - 1 < chunks))
        def _():
            corner(k - 1)

        done = k - 2

        @pl.when(done >= 0)
        def _():
            finish(done)

        for h in range(hops):
            @pl.when(k == h + 1)
            def _():
                hop(h).wait()
                cnt[h + 1] = cnt[h] + cnt_in[h]
                if h + 1 < hops:
                    hop(h + 1).start()

        @pl.when((done >= 0) & (done < 3))
        def _():
            project(done)

        for m in (1, 2):
            @pl.when(done == m)
            def _():
                kv_send(m).start()

        @pl.when((done >= 4) & (done < 4 + per))
        def _():
            upward(done - 4)

        @pl.when(k == first_att)
        def _():
            for m in (1, 2):
                kv_send(m).wait()
            writes[3].start()
            writes[4].start()
            writes[5].start()
            writes[1].wait()

        @pl.when((k >= first_att) & (k < first_att + pairs // each))
        def _():
            def pair(i, carry):
                attend((k - first_att) * each + i)
                return carry

            lax.fori_loop(0, each, pair, 0)

        @pl.when(k == first_att + pairs // each)
        def _():
            writes[6].start()
            writes[9].start()
            branch()
            writes[7].start()
            writes[8].start()

        @pl.when(done >= 4 + per)
        def _():
            feed(done - 4 - per)

        return carry

    lax.fori_loop(0, chunks + 2, tick, 0)
    count = cnt[hops]
    weight = rows * (1 << hops) / count
    scale_ref[...] = weight
    writes[0].wait()
    some = 128

    def loss(i, carry):
        at = pl.ds(pl.multiple_of(i * some, some), some)
        bias = par_ref[0:1, pl.ds(pl.multiple_of(8 * width + hidden + i * some, some), some)]
        out_y = x_ref[:, at].astype(F32) + (fy[:, at] + bias)
        g = weight[0:1, :] * valid_ref[...] * (out_y - t_ref[:, at].astype(F32))
        low = g.astype(BF16)
        fy[:, at] = g
        n1[:, at] = low
        n1t[i] = low.T
        sum_ref[0:1, at] = jnp.sum(low.astype(F32), axis=0, keepdims=True)
        return carry

    lax.fori_loop(0, width // some, loss, 0)
    for k in (10, 11, 12):
        writes[k].start()
    for k in range(2, 13):
        if k != 1:
            writes[k].wait()

    def drain(c, carry):
        w_copy(c).wait()
        return carry

    lax.fori_loop(0, chunks, drain, 0)


def forward_pass(master, vec, tokens, targets, valid, seg, replicas, total):
    rows, width = tokens.shape
    half = rows // 2
    stack = master.shape[1]
    chunks = stack // CHUNK
    hidden = (stack - 4 * width) // 2
    replica_bits = replicas.bit_length() - 1
    assert replicas == 1 << replica_bits
    blocks = width // BS
    hops = 3 + replica_bits
    anyspace = pl.BlockSpec(memory_space=pl.ANY)
    vmem = pl.BlockSpec(memory_space=pltpu.VMEM)
    dma = pltpu.SemaphoreType.DMA
    turned = sds((blocks, BS, rows), BF16)
    flat = sds((rows, width), BF16)
    two = sds((2, rows, width), BF16)
    tall = sds((rows, hidden), BF16)
    return pl.pallas_call(
        partial(fwd_kernel, total, replica_bits),
        out_shape=[
            sds((blocks, BS, stack), BF16), turned, turned, turned, turned, flat, two, two, flat, tall, tall,
            sds((rows, width), F32), flat, sds((3, rows, LANES), F32),
            sds((blocks, 2, rows), F32), sds((1, width), F32), sds((1, total), F32), sds((8, LANES), F32),
        ],
        in_specs=[anyspace] + [vmem] * 5,
        out_specs=[anyspace] * 14 + [vmem] * 4,
        scratch_shapes=[
            pltpu.VMEM((blocks, BS, stack), BF16),
            pltpu.VMEM((3, BS, CHUNK), F32),
            pltpu.VMEM((8, 16, LANES), F32),
            pltpu.VMEM((rows, width), BF16),
            pltpu.VMEM((rows, width), BF16),
            pltpu.VMEM((blocks, BS, rows), BF16),
            pltpu.VMEM((blocks, BS, rows), BF16),
            pltpu.VMEM((3, rows, width), BF16),
            pltpu.VMEM((2, rows, width), BF16),
            pltpu.VMEM((rows, hidden), BF16),
            pltpu.VMEM((rows, hidden), BF16),
            pltpu.VMEM((rows, width), BF16),
            pltpu.VMEM((rows, width), F32),
            pltpu.VMEM((5, rows, half), F32),
            pltpu.VMEM((2, rows, LANES), F32),
            pltpu.VMEM((2, rows, 2 * LANES), F32),
            pltpu.VMEM((5, half, half), F32),
            pltpu.VMEM((2 * rows, LANES), BF16),
            pltpu.VMEM((2 * rows, 2 * LANES), BF16),
            pltpu.VMEM((3, rows, LANES), F32),
            pltpu.VMEM((hops + 1, 8, LANES), F32),
            pltpu.VMEM((hops, 8, LANES), F32),
            dma((3,)), dma((chunks,)), dma((8, chunks)), dma((8, chunks)), dma((7,)), dma((7,)),
            dma((2,)), dma((2,)), dma((hops,)), dma((hops,)), dma((13,)),
        ],
        compiler_params=pltpu.CompilerParams(
            collective_id=1, has_side_effects=True, vmem_limit_bytes=59 * MIB
        ),
    )(master, vec, tokens, targets, valid, seg)


def update_kernel(f_ref, g_ref, ls_ref, rs_ref, lr_ref, rr_ref, m_ref, nl_ref, nr_ref, nm_ref, mc_ref):
    factor = f_ref[0, 0]
    half_sq = 0.5 * factor * factor
    for k in range(ls_ref.shape[1]):
        at = slice(k * BS, (k + 1) * BS)
        g = g_ref[:, at]
        gt = g.T
        nl_ref[0, k] = 0.5 * ls_ref[0, k] + half_sq * dot(g, gt)
        nr_ref[0, k] = 0.5 * rs_ref[0, k] + half_sq * dot(gt, g)
        tb = (g.astype(F32) * factor).astype(BF16)
        mb = dot(lr_ref[0, k], tb).astype(BF16)
        new = m_ref[:, at] - LEARN * dot(mb, rr_ref[0, k])
        nm_ref[:, at] = new
        mc_ref[:, at] = new.astype(BF16)


def update(factor, g, ls, rs, lr, rr, m):
    rows, total = g.shape
    count = ls.shape[1]
    per = 8
    blk = pl.BlockSpec((1, per, BS, BS), lambda j: (0, j, 0, 0))
    col = pl.BlockSpec((rows, per * BS), lambda j: (0, j))
    return call(
        update_kernel,
        (count // per,),
        [pl.BlockSpec(memory_space=pltpu.SMEM), col, blk, blk, blk, blk, col],
        [blk, blk, col, col],
        [sds(ls.shape, F32), sds(rs.shape, F32), sds(m.shape, F32), sds(m.shape, BF16)],
        cost=cost(8 * rows * total * BS, rows * total * 32),
    )(factor, g, ls, rs, lr, rr, m)


PAIR = 1024
TILE = PAIR // 2


def bwd_kernel(plan, levels, replica_bits, lines, *refs):
    groups = len(plan)
    pairs = sum(plan)
    at_refs = refs[:groups]
    (hb_ref, gb_ref, dg_ref, w_ref, q_ref, kv_ref, kvo_ref, ob_ref, gy_ref, x_ref, tab_ref,
     lse_ref, par_ref, gbs_ref, seg_ref,
     g_out, in_out, bo, vec_out, sq_out,
     a_own, a_oth, b_own, b_oth, s1, r1, r2, zs, gb, gub, gob, gqkv, wr, att, mask, kpos, vpos, dkpos, dvpos, dqs, qcat, gcat,
     rowsum, own_kv, snd_kv, rcv_kv, tab, gn1, gn2, gy, xs, vg, gus, qs, v, vr, vd, sq, sq_in,
     sem_l, sem_b, sem_as, sem_ar, sem_bs, sem_br, sem_1s, sem_1r, sem_2s, sem_2r,
     sem_zs, sem_zr, sem_gs, sem_gr, sem_vs, sem_vr, sem_qs, sem_qr, sem_o, sem_w, sem_t, sem_i, sem_ks, sem_kr) = refs[groups:]
    rows, width = gb.shape
    half = rows // 2
    hidden = gub.shape[1]
    s = lax.axis_index("shard")
    z = lax.axis_index("dp")
    core, x, y = bits_of(s, 3)
    parity = core
    zb = bits_of(z, replica_bits)
    to_core = {"shard": s + 1 - 2 * core}
    to_x = {"shard": s + 2 - 4 * x}
    to_y = {"shard": s + 4 - 8 * y}
    to_z = [{"dp": z + (1 - 2 * zb[l]) * (1 << l)} for l in range(replica_bits)]
    peers = [to_core, to_x, to_y] + to_z
    first = [sum(plan[:k]) for k in range(groups + 1)]
    last = first[3]

    def local(k, src, dst):
        return pltpu.make_async_copy(src, dst, sem_i.at[k])

    loads = [
        local(0, gb_ref, gb), local(1, dg_ref, gub), local(2, tab_ref, tab), local(3, gy_ref, gy), local(4, x_ref, xs),
    ]

    def cols(c):
        return pl.ds(pl.multiple_of(c * PAIR, PAIR), PAIR)

    chunks_qkv = plan[3]
    per = plan[2]

    def w_load(c, slot):
        return pltpu.make_async_copy(w_ref.at[:, :, cols(c)], wr.at[slot], sem_w.at[slot])

    down0 = chunks_qkv + 1 + per
    up0 = chunks_qkv + 1

    def att_load(p, k):
        lanes = pl.ds(pl.multiple_of(p * LANES, LANES), LANES)
        src = (
            q_ref.at[:, lanes], kv_ref.at[0, :, lanes], kv_ref.at[1, :, lanes],
            kvo_ref.at[0, :, lanes], kvo_ref.at[1, :, lanes], ob_ref.at[:, lanes],
        )[k]
        return pltpu.make_async_copy(src, att.at[p % 2, k], sem_t.at[p % 2, k])

    def a_local(k):
        return pltpu.make_async_copy(at_refs[k].at[:, core], a_own.at[k], sem_l.at[k])

    def a_send(k):
        return remote(at_refs[k].at[:, 1 - core], a_oth.at[k], sem_as.at[k], sem_ar.at[k], to_core)

    def b_src(k, i):
        off = cols(i - first[k])
        return (hb_ref.at[:, off], gb_ref, gub.at[:, off], gqkv.at[:, off])[k]

    def b_send(k, i):
        return remote(b_src(k, i), bo.at[i], sem_bs.at[i], sem_br.at[i], to_core)

    def by_group(i, act):
        for k in range(groups):
            @pl.when((i >= first[k]) & (i < first[k + 1]))
            def _():
                act(k)

    def fetch(i):
        slot = i % 2

        def act(k):
            b_send(k, i).wait()
            pltpu.make_async_copy(b_src(k, i), b_own.at[slot], sem_b.at[0, slot]).start()
            pltpu.make_async_copy(bo.at[i], b_oth.at[slot], sem_b.at[1, slot]).start()

        by_group(i, act)

    w_load(chunks_qkv, 2).start()
    loads[0].start()
    w_load(down0, 0).start()
    w_load(up0, 1).start()
    loads[1].start()
    loads[2].start()
    for k in range(6):
        att_load(0, k).start()
    meet(peers)
    for k in range(groups):
        a_local(k).start()
        a_send(k).start()
        if k == 0:
            for i in range(plan[0]):
                b_send(0, i).start()
        if k == 1:
            b_send(1, first[1]).start()
    loads[3].start()
    loads[4].start()

    first_row = 4 * (s // 2)

    def see(t, carry):
        b, j = key_tile(t, parity)
        quarter = jnp.where(b == 0, parity, 3 - parity)
        qrow = first_row + 2 * parity + b
        krow = first_row + jnp.where(j == 0, 0, jnp.where(j == 3, 1, j + 1))
        kseg = column(seg_ref[krow])
        for g in range(half // LANES):
            qseg = seg_ref[qrow][:, g * LANES : (g + 1) * LANES].astype(F32)
            kp = j * half + lax.broadcasted_iota(jnp.int32, (half, LANES), 0)
            qp = quarter * half + g * LANES + lax.broadcasted_iota(jnp.int32, (half, LANES), 1)
            mask[t, :, g * LANES : (g + 1) * LANES] = jnp.where((kp <= qp) & (kseg == qseg), BIG, NEG)
        return carry

    def copy1(i, t):
        slot = i % 2
        src = s1.at[slot, t, :, 1 - x] if t == 0 else s1.at[slot, t, 1 - y]
        return remote(src, r1.at[i, t], sem_1s.at[i, t], sem_1r.at[i, t], to_x if t == 0 else to_y)

    def copy2(i, t):
        bit = y if t == 0 else x
        return remote(
            r1.at[i, t, 1 - bit], r2.at[i, :, t * TILE : (t + 1) * TILE],
            sem_2s.at[i, t], sem_2r.at[i, t], to_y if t == 0 else to_x,
        )

    starts = [0]
    for l in range(levels):
        starts.append(starts[l] + (BS >> (l + 1)))

    def z_rows(l):
        return pl.ds(starts[l], BS >> (l + 1))

    def level_src(i, l, which):
        size = BS >> (l + 1)
        off = pl.multiple_of(which * size, size)
        if l == 0:
            return r2.at[i, pl.ds(off, size)]
        return zs.at[i, pl.ds(pl.multiple_of(starts[l - 1] + off, size), size)]

    def copy_z(i, l):
        return remote(
            level_src(i, l, 1 - zb[l]), zs.at[i, z_rows(l)], sem_zs.at[i, l], sem_zr.at[i, l], to_z[l]
        )

    def g_rows(l):
        base = sum((zb[m] * (BS >> (m + 1)) for m in range(l + 1)), 0)
        size = BS >> (l + 1)
        return pl.ds(pl.multiple_of(base, size), size)

    def copy_g(i, l):
        return remote(r2.at[i, g_rows(l)], r2.at[i, g_rows(l)], sem_gs.at[i, l], sem_gr.at[i, l], to_z[l])

    def out_copy(i):
        spot = pairs - first[1] + i
        spot = jnp.where(i >= first[1], i - first[1] + plan[3], spot)
        spot = jnp.where(i >= first[3], i - first[3], spot)
        return pltpu.make_async_copy(r2.at[i], g_out.at[:, cols(spot)], sem_o.at[i])

    def stage_a(i):
        slot = i % 2
        group = sum((jnp.where(i >= first[k], 1, 0) for k in range(1, groups)), 0)
        for k in range(groups):
            @pl.when(i == first[k])
            def _():
                a_local(k).wait()
                a_send(k).wait()

        pltpu.make_async_copy(bo.at[i], b_own.at[slot], sem_b.at[0, slot]).wait()
        pltpu.make_async_copy(bo.at[i], b_oth.at[slot], sem_b.at[1, slot]).wait()
        size = 4 * BS
        own = a_own[group].reshape(size, rows)
        oth = a_oth[group].reshape(size, rows)
        for t in range(2):
            at = slice(t * TILE, (t + 1) * TILE)
            acc = dot(own, b_own[slot, :, at]) + dot(oth, b_oth[slot, :, at])
            s1[slot, t] = acc.astype(BF16).reshape(2, 2, BS, TILE)
            copy1(i, t).start()

    def stage_b(i):
        slot = i % 2
        for t in range(2):
            copy1(i, t).wait()
            kept = s1[slot, t, :, x] if t == 0 else s1[slot, t, y]
            r1[i, t] = (r1[i, t].astype(F32) + kept.astype(F32)).astype(BF16)
            copy2(i, t).start()

    def stage_c(i):
        for t in range(2):
            copy2(i, t).wait()
            at = slice(t * TILE, (t + 1) * TILE)
            bit = y if t == 0 else x
            r2[i, :, at] = (r2[i, :, at].astype(F32) + r1[i, t, bit].astype(F32)).astype(BF16)
        if levels:
            copy_z(i, 0).start()
        else:
            out_copy(i).start()

    def stage_z(l):
        def run(i):
            copy_z(i, l).wait()
            total = zs[i, z_rows(l)].astype(F32) + level_src(i, l, zb[l])[...].astype(F32)
            if l + 1 < levels:
                zs[i, z_rows(l)] = total.astype(BF16)
                copy_z(i, l + 1).start()
            else:
                r2[i, g_rows(l)] = total.astype(BF16)
                copy_g(i, l).start()
        return run

    def stage_g(l):
        def run(i):
            copy_g(i, l).wait()
            if l:
                copy_g(i, l - 1).start()
            else:
                part = r2[i].astype(F32)
                part = jnp.sum((part * part).reshape(BS // 8, 8, PAIR), axis=0)
                sq[0] += sum(part[:, g * LANES : (g + 1) * LANES] for g in range(PAIR // LANES))
                out_copy(i).start()
        return run

    sub = 512

    def attention_grad():
        loads[0].wait()
        w_load(0, 2).wait()
        for i in range(width // sub):
            tall = wr[2, i * (sub // BS) : (i + 1) * (sub // BS)].reshape(sub, width)
            gob[:, i * sub : (i + 1) * sub] = dot_nt(gb[...], tall).astype(BF16)
        w_load(2, 2).start()
        loads[1].wait()
        loads[2].wait()
        gn2[...] = jnp.zeros_like(gn2)
        gn1[...] = jnp.zeros_like(gn1)

    def feed_grad(k):
        w_load(0, 0).wait()
        w_load(0, 1).wait()

        def part(i, carry):
            inner = pl.ds(pl.multiple_of(i * sub, sub), sub)
            at = pl.ds(pl.multiple_of(k * PAIR + i * sub, sub), sub)
            act = dot(gb[...], wr[0, :, :, inner].reshape(width, sub))
            low = (act * gub[:, at].astype(F32)).astype(BF16)
            gub[:, at] = low
            gus[0:1, at] = jnp.sum(low.astype(F32), axis=0, keepdims=True)
            gn2[...] += dot_nt(low, wr[1, :, :, inner].reshape(width, sub))
            return carry

        lax.fori_loop(0, PAIR // sub, part, 0)
        b_send(2, first[2] + k).start()
        more = k + 1 < per
        w_load(jnp.where(more, down0 + k + 1, 0), 0).start()
        w_load(jnp.where(more, up0 + k + 1, 1), 1).start()

    scale = HD**-0.5

    def attend(p):
        slot = p % 2
        for k in range(6):
            att_load(p, k).wait()

        @pl.when(p + 1 < width // LANES)
        def _():
            for k in range(6):
                att_load(p + 1, k).start()

        lanes = pl.ds(pl.multiple_of(p * LANES, LANES), LANES)
        place_keys(att.at[slot, 1], att.at[slot, 3], kpos, parity)
        place_keys(att.at[slot, 2], att.at[slot, 4], vpos, parity)
        dkpos[...] = jnp.zeros_like(dkpos)
        dvpos[...] = jnp.zeros_like(dvpos)
        dqs[...] = jnp.zeros_like(dqs)
        for b in range(2):
            at = slice(b * half, (b + 1) * half)
            qcat[b] = split_heads(att[slot, 0, at, :] * jnp.asarray(scale, BF16))
            gs = gob[at, lanes]
            gcat[b] = split_heads(gs)
            prod = (gs.astype(F32) * att[slot, 5, at, :].astype(F32)).T
            rowsum[b, 0:1, :half] = lse_ref[p, 0:1, at]
            rowsum[b, 0:1, half:] = lse_ref[p, 1:2, at]
            rowsum[b, 1:2, :half] = jnp.sum(prod[:HD, :], axis=0, keepdims=True)
            rowsum[b, 1:2, half:] = jnp.sum(prod[HD:, :], axis=0, keepdims=True)

        def tile(t, carry):
            b, j = key_tile(t, parity)
            ks = pl.ds(pl.multiple_of(j * half, half), half)
            keys = kpos[ks, :]
            qh, gh = qcat[b], gcat[b]
            m = mask[t]
            got = dot_nt(keys, qh)
            got = jnp.concatenate([jnp.minimum(got[:, :half], m), jnp.minimum(got[:, half:], m)], axis=1)
            prob = jnp.exp(got - rowsum[b, 0:1, :])
            dp = dot_nt(vpos[ks, :], gh)
            ds = (prob * (dp - rowsum[b, 1:2, :])).astype(BF16)
            dvpos[ks, :] += dot(prob.astype(BF16), gh)
            dkpos[ks, :] += dot(ds, qh)
            dqs[b] += dot(ds, keys, ((0,), (0,)))
            return carry

        lax.fori_loop(0, 5, tile, 0)
        for b in range(2):
            at = slice(b * half, (b + 1) * half)
            dq = join_heads(dqs[b]) * scale
            gqkv[at, lanes] = turn(dq, tab[0, at, :], -tab[1, at, :], -tab[2, at, :]).astype(BF16)
        for k, src in enumerate((dkpos, dvpos)):
            for b in range(2):
                at = slice(b * half, (b + 1) * half)
                mine = parity if b == 0 else 3 - parity
                other = 1 - parity if b == 0 else 2 + parity
                own_kv[slot, k, at, :] = src[pl.ds(pl.multiple_of(mine * half, half), half), :]
                snd_kv[slot, k, at, :] = src[pl.ds(pl.multiple_of(other * half, half), half), :].astype(BF16)
        kv_back(p).start()

    def kv_back(p):
        return remote(snd_kv.at[p % 2], rcv_kv.at[p], sem_ks.at[p], sem_kr.at[p], to_core)

    def settle(p):
        kv_back(p).wait()
        slot = p % 2
        key = own_kv[slot, 0] + rcv_kv[p, 0].astype(F32)
        gqkv[:, pl.ds(pl.multiple_of(width + p * LANES, LANES), LANES)] = turn(key, tab[0], -tab[1], -tab[2]).astype(BF16)
        value = own_kv[slot, 1] + rcv_kv[p, 1].astype(F32)
        gqkv[:, pl.ds(pl.multiple_of(2 * width + p * LANES, LANES), LANES)] = value.astype(BF16)

    def qkv_grad(m):
        w_load(0, m).wait()
        part = gqkv[:, cols(m)]
        qs[0:1, cols(m)] = jnp.sum(part.astype(F32), axis=0, keepdims=True)
        for i in range(width // sub):
            tall = wr[m, i * (sub // BS) : (i + 1) * (sub // BS)].reshape(sub, PAIR)
            gn1[:, i * sub : (i + 1) * sub] += dot_nt(part, tall)

    in_copy = pltpu.make_async_copy(gy, in_out, sem_i.at[5])

    def norm_grad():
        loads[3].wait()
        loads[4].wait()
        step = 64
        vg[...] = jnp.zeros_like(vg)

        def chunk(i, carry):
            at = pl.ds(pl.multiple_of(i * step, step), step)
            xh, rstd = normed(xs[at, :].astype(F32))
            total = gy[at, :]
            sums = []
            for g_n, gain in ((gn1[at, :], par_ref[0:1, 0:width]), (gn2[at, :], par_ref[0:1, 2 * width : 3 * width])):
                sums.append(jnp.sum(g_n * xh, axis=0, keepdims=True))
                sums.append(jnp.sum(g_n, axis=0, keepdims=True))
                e = g_n * gain
                mean = jnp.mean(e, axis=-1, keepdims=True)
                along = jnp.mean(e * xh, axis=-1, keepdims=True)
                total = total + rstd * (e - mean - xh * along)
            gy[at, :] = total
            vg[...] += jnp.concatenate(sums, axis=0)
            return carry

        lax.fori_loop(0, rows // step, chunk, 0)
        in_copy.start()
        v[...] = jnp.zeros_like(v)
        pieces = [(vg, r, width) for r in range(4)] + [(qs, 0, 3 * width), (gbs_ref, 0, width), (gus, 0, hidden), (gbs_ref, 0, width)]
        spot = 0
        for ref, r, size in pieces:
            for g in range(size // LANES):
                owner, line = spot // lines, spot % lines
                v[owner // 4, (owner // 2) % 2, owner % 2, line : line + 1, :] = ref[r : r + 1, g * LANES : (g + 1) * LANES]
                spot += 1
        v_copy(0).start()

    vecs = [
        (v.at[:, :, 1 - core], vr.at[0, :, :], to_core),
        (vr.at[0, :, 1 - x], vr.at[1, 0, :], to_x),
        (vr.at[1, 0, 1 - y], vr.at[1, 1, 0], to_y),
    ]

    def v_copy(k):
        if k < 3:
            src, dst, peer = vecs[k]
        else:
            src, dst, peer = vd.at[2 * (k - 3)], vd.at[2 * (k - 3) + 1], to_z[k - 3]
        return remote(src, dst, sem_vs.at[k], sem_vr.at[k], peer)

    def v_done(k):
        v_copy(k).wait()
        if k == 0:
            vr[0] = vr[0] + v[:, :, core]
        elif k == 1:
            vr[1, 0] = vr[1, 0] + vr[0, :, x]
        else:
            if k == 2:
                total = vr[1, 1, 0] + vr[1, 0, y]
            else:
                total = vd[2 * (k - 3)] + vd[2 * (k - 3) + 1]
            vd[2 * (k - 2)] = total

    v_hops = 3 + replica_bits
    sq[...] = jnp.zeros_like(sq)
    stages = [stage_a, stage_b, stage_c]
    stages += [stage_z(l) for l in range(levels)] + [stage_g(l) for l in reversed(range(levels))]
    lags = len(stages)
    att_pairs = width // LANES
    fetch(0)
    lax.fori_loop(0, 5, see, 0)

    def step(i, carry):
        @pl.when(i == last)
        def _():
            settle(att_pairs - 1)
            for m in range(plan[3]):
                b_send(3, last + m).start()
            fetch(last)

        for lag, stage in enumerate(stages):
            @pl.when((i >= lag) & (i < pairs + lag))
            def _():
                stage(i - lag)

            if lag == 0:
                @pl.when((i + 1 < pairs) & (i + 1 != last))
                def _():
                    fetch(i + 1)

        @pl.when(i == 0)
        def _():
            attention_grad()

        @pl.when(i < per)
        def _():
            feed_grad(i)

        @pl.when((i >= 2) & (i - 2 < att_pairs - 1))
        def _():
            settle(i - 2)

        @pl.when((i >= 1) & (i - 1 < att_pairs))
        def _():
            attend(i - 1)

        for m in range(plan[3]):
            @pl.when(i == last + m)
            def _():
                qkv_grad(m)

        @pl.when(i == pairs)
        def _():
            norm_grad()

        for k in range(v_hops):
            @pl.when(i == pairs + k + 1)
            def _():
                v_done(k)
                if k + 1 < v_hops:
                    v_copy(k + 1).start()
        return carry

    lax.fori_loop(0, pairs + max(lags - 1, v_hops + 1), step, 0)
    total = vd[2 * replica_bits]
    vec_out[...] = total
    real = lax.broadcasted_iota(jnp.int32, total.shape, 0) < lines
    square = jnp.where(real, total * total, 0.0)
    sq[0] += square[0:8] + square[8:16]
    for k, peer in enumerate((to_core, to_x, to_y)):
        hop = remote(sq.at[k], sq_in.at[k], sem_qs.at[k], sem_qr.at[k], peer)
        hop.start()
        hop.wait()
        sq[k + 1] = sq[k] + sq_in[k]
    sq_out[...] = sq[3]
    in_copy.wait()

    def drain(i, carry):
        out_copy(i).wait()
        return carry

    lax.fori_loop(0, pairs, drain, 0)


def backward_pass(ats, hb, gb, dg, weights, q, kv, kvo, ob, gy, x, tables, lse, params, gb_sum, seg, replicas, lines):
    rows, width = gb.shape
    half = rows // 2
    hidden = hb.shape[1]
    plan = [hidden // PAIR, width // PAIR, hidden // PAIR, 3 * width // PAIR]
    pairs = sum(plan)
    groups = len(plan)
    replica_bits = replicas.bit_length() - 1
    levels = replica_bits if replicas <= 8 else 0
    dma = pltpu.SemaphoreType.DMA
    lv, vh = max(levels, 1), 3 + replica_bits
    att_pairs = width // LANES
    blocks = width // BS
    vm = pltpu.VMEM
    scratch = [
        vm((groups, 4, BS, rows), BF16), vm((groups, 4, BS, rows), BF16),
        vm((2, rows, PAIR), BF16), vm((2, rows, PAIR), BF16),
        vm((2, 2, 2, 2, BS, TILE), BF16), vm((pairs, 2, 2, BS, TILE), BF16),
        vm((pairs, BS, PAIR), BF16), vm((pairs, max(BS - (BS >> levels), 16), PAIR), BF16),
        vm((rows, width), BF16), vm((rows, hidden), BF16), vm((rows, width), BF16), vm((rows, 3 * width), BF16),
        vm((3, blocks, BS, PAIR), BF16),
        vm((2, 6, rows, LANES), BF16), vm((5, half, half), F32),
        vm((2 * rows, LANES), BF16), vm((2 * rows, LANES), BF16), vm((2 * rows, LANES), F32), vm((2 * rows, LANES), F32),
        vm((2, rows, LANES), F32), vm((2, rows, LANES), BF16), vm((2, rows, LANES), BF16), vm((2, 8, rows), F32),
        vm((2, 2, rows, LANES), F32), vm((2, 2, rows, LANES), BF16), vm((att_pairs, 2, rows, LANES), BF16),
        vm((3, rows, LANES), F32), vm((rows, width), F32), vm((rows, width), F32), vm((rows, width), F32),
        vm((rows, width), BF16), vm((4, width), F32), vm((1, hidden), F32), vm((1, 3 * width), F32),
        vm((2, 2, 2, 16, LANES), F32), vm((2, 2, 2, 16, LANES), F32), vm((2 * replica_bits + 2, 16, LANES), F32),
        vm((4, 8, LANES), F32), vm((3, 8, LANES), F32),
        dma((groups,)), dma((2, 2)), dma((groups,)), dma((groups,)), dma((pairs,)), dma((pairs,)),
        dma((pairs, 2)), dma((pairs, 2)), dma((pairs, 2)), dma((pairs, 2)),
        dma((pairs, lv)), dma((pairs, lv)), dma((pairs, lv)), dma((pairs, lv)),
        dma((vh,)), dma((vh,)), dma((3,)), dma((3,)), dma((pairs,)), dma((3,)), dma((2, 6)), dma((6,)),
        dma((att_pairs,)), dma((att_pairs,)),
    ]
    anyspace = pl.BlockSpec(memory_space=pl.ANY)
    vmem = pl.BlockSpec(memory_space=pltpu.VMEM)
    return pl.pallas_call(
        partial(bwd_kernel, plan, levels, replica_bits, lines),
        out_shape=[
            sds((BS, pairs * PAIR), BF16), sds((rows, width), F32), sds((pairs, rows, PAIR), BF16),
            sds((16, LANES), F32), sds((8, LANES), F32),
        ],
        in_specs=[anyspace] * (groups + 11) + [vmem] * 4,
        out_specs=[anyspace] * 3 + [vmem] * 2,
        scratch_shapes=scratch,
        compiler_params=pltpu.CompilerParams(
            collective_id=0, has_side_effects=True, vmem_limit_bytes=60 * MIB
        ),
    )(
        *[a.reshape(4, 2, BS, rows) for a in ats], hb, gb, dg, weights, q, kv, kvo, ob, gy, x, tables,
        lse, params, gb_sum, seg,
    )


def body(
    tokens, targets, segments, valid, master, vectors, left_stat, right_stat, left_root, right_root, vector_stat,
):
    rows, width = tokens.shape
    stack = master.shape[1]
    half = rows // 2
    shards = lax.axis_size("shard")
    replicas = lax.axis_size("dp")
    own_len = vectors.shape[0]
    lines = own_len // LANES
    vec = jnp.pad(vectors.reshape(lines, LANES), ((0, 16 - lines), (0, 0)))
    seg = segments.reshape(-1, 1, half)
    (weights, n1t, n2t, obt, gbt, q, kv, kvo, ob, hb, dg, gy, gb, tables, lse, gb_sum, params, _) = forward_pass(
        master, vec, tokens, targets, valid.astype(F32).reshape(rows, 1), seg, replicas, own_len * shards
    )
    grads, input_grad, _, vec_total, squares = backward_pass(
        (gbt, obt, n2t, n1t), hb, gb, dg, weights, q, kv, kvo, ob, gy, tokens, tables, lse, params, gb_sum, seg,
        replicas, lines,
    )
    own_vector = vec_total[:lines].reshape(own_len)
    if replicas <= 8:
        square_sum = jnp.sum(squares)
    else:
        grads = lax.psum_scatter(grads, "dp", scatter_dimension=1, tiled=True)
        grads = lax.all_gather(grads, "dp", axis=1, tiled=True)
        square_sum = jnp.sum(squares) + lax.psum(jnp.sum(jnp.square(grads.astype(F32))), "shard")
    grad_norm = jnp.sqrt(square_sum)
    factor = jnp.minimum(1.0, math.sqrt(width * stack / BS) / grad_norm)
    new_left, new_right, new_master, master_copy = update(
        factor.reshape(1, 1), grads, left_stat, right_stat, left_root, right_root, master
    )
    scaled_vec = own_vector * factor
    new_vstat = 0.5 * vector_stat + 0.5 * scaled_vec * scaled_vec
    new_vectors = vectors - LEARN_VEC * scaled_vec / jnp.sqrt(new_vstat)
    return (input_grad, grad_norm, new_left, new_right, new_master, master_copy, new_vectors, new_vstat)


def solution(mesh):
    rows = P(("dp", "shard"), None)
    quad = P("shard", None, None, None)
    return jax.shard_map(
        body,
        mesh=mesh,
        in_specs=(
            rows, rows, P("dp"), P(("dp", "shard")), P("shard", None), P("shard"), quad, quad, quad, quad, P("shard"),
        ),
        out_specs=(rows, P(), quad, quad, P("shard", None), P("shard", None), P("shard"), P("shard")),
        check_vma=False,
    )
```
